128 devices in a mesh: gx: 16 (over y, z), gy: 8 (over x, core).
Axes of the slice: x: 4, y: 4, z: 4, core: 2. Of those that a mesh axis runs over, the one named last changes fastest.
Arguments:
- features: float32 [2048, 64, 512], P(('gx', 'gy')), may hold values from -6 to 6
- send_pick: int32 [128, 32], P(('gx', 'gy')), may hold values from -1 to 15, as said below
- occupancy: int32 [4096, 512], P(('gx', 'gy')), may hold values from 0 to 1, as said below
- neighbours: int32 [4096, 6], P(('gx', 'gy')), may hold values from -1 to 4095, as said below
- weight_one: float32 [3, 3, 3, 64, 64], replicated, may hold values from -0.25 to 0.25
- bias_one: float32 [64], replicated, may hold values from -3 to 3
Outputs:
- block_out: float32 [4096, 64, 512], P(('gx', 'gy'))
The draws below stay inside these ranges and needn't reach their ends.
Inputs may be any that keep to these rules, and one draw needn't show every extreme that they name: `send_pick`: entry j of a source device's row names the source row (0 to 15) sent to owner gx index j // 2 in place j % 2, or -1 for nothing; every source row is named exactly once; a source sends only to owners with its own gy index, at most 2 bricks to one owner; in every gy column some owner receives 2 bricks from every source. `occupancy`: 1 where a voxel of an owner brick slot is occupied; slots that receive no brick are all 0. Entry d of a slot is the global slot (owner rank times 32 plus slot) of the brick beside it across its -x, +x, -y, +y, -z or +z face, or -1; the relation is mutual; -y, +y, -z and +z neighbours have the same owner; -x and +x neighbours have the same owner or the owner of rank one lower (-x) or one higher (+x); empty slots have no neighbours and are no one's neighbour.
All inputs are finite; a program needn't handle non-finite values.
Results may differ from the reference program's by a relative error of at most 0.000062.
Values sent between devices are 32-bit elements; how exact they have to be, the bound alone decides.
No kernel may reach another device: no remote copies, remote signals or barrier semaphores. Data moves between devices by JAX's collectives and lax.ppermute only.
A program may use at most 128 MiB of HBM per device.

```python
import jax
import jax.numpy as jnp
from jax import lax

C = 64
EDGE = 8
MOST = 2
RX = 2
RY = 4
RZ = 8
V = 512
TILE_PLACES = 32
SRC = 16
BRICKS = 4096
SOURCES = 2048
N_GX = 16
N_GY = 8
DEVICES = 128


def brick_layout(key):
    base = jax.random.fold_in(key, 11)
    keys = jax.random.split(base, 7)
    keeper_preference = jax.random.randint(keys[0], (N_GY, N_GX), 0, 5)
    full_owner = jax.random.randint(keys[1], (N_GY,), 0, N_GX)
    owner_ids = jnp.arange(N_GX, dtype=jnp.int32)
    keeper_preference = keeper_preference + 16 * (owner_ids[None, :] == full_owner[:, None]).astype(jnp.int32)
    noise_perturbation = jax.vmap(lambda one: jax.random.permutation(one, TILE_PLACES))(jax.random.split(keys[2], N_GY * N_GX))
    noise_perturbation = noise_perturbation.reshape(N_GY, N_GX, TILE_PLACES).astype(jnp.int32)
    place_occupant = jnp.arange(TILE_PLACES, dtype=jnp.int32) // MOST
    sender_positions = jnp.arange(N_GX, dtype=jnp.int32)[:, None]
    keeper_reward = 8 * ((place_occupant[None, :] == sender_positions) | (place_occupant[None, :] == (sender_positions + 1) % N_GX)).astype(jnp.int32)
    place_rating = (keeper_preference[:, place_occupant][:, None, :] + keeper_reward[None, :, :]) * TILE_PLACES + noise_perturbation
    top_values, chosen = lax.top_k(place_rating, SRC)
    row_order = jax.vmap(lambda one: jax.random.permutation(one, SRC))(jax.random.split(keys[3], N_GY * N_GX))
    row_order = row_order.reshape(N_GY, N_GX, SRC).astype(jnp.int32)
    match = chosen[:, :, :, None] == jnp.arange(TILE_PLACES, dtype=jnp.int32)[None, None, None, :]
    picked = jnp.sum(jnp.where(match, row_order[:, :, :, None] + 1, 0), axis=2) - 1
    send_pick = jnp.transpose(picked, (1, 0, 2)).reshape(DEVICES, TILE_PLACES).astype(jnp.int32)
    sent = (picked >= 0).reshape(N_GY, N_GX, N_GX, MOST)
    filled = jnp.transpose(sent, (2, 0, 1, 3)).reshape(DEVICES, TILE_PLACES)
    cells = RX * RY * RZ
    cell_ids = jnp.arange(cells, dtype=jnp.int32)
    slot_ids = jnp.arange(TILE_PLACES, dtype=jnp.int32)
    cell_rank = jax.vmap(lambda one: jax.random.permutation(one, cells))(jax.random.split(keys[4], DEVICES)).astype(jnp.int32)
    cell_key = jnp.where(cell_ids[None, :] == 0, -2, jnp.where(cell_ids[None, :] == (RX - 1) * RY * RZ, -1, cell_rank))
    cell_seq = jnp.argsort(cell_key, axis=1).astype(jnp.int32)
    slot_key = (1 - filled.astype(jnp.int32)) * TILE_PLACES + slot_ids[None, :]
    slot_seq = jnp.argsort(slot_key, axis=1).astype(jnp.int32)
    slot_pos = jnp.argsort(slot_seq, axis=1).astype(jnp.int32)
    place = jnp.take_along_axis(cell_seq, slot_pos, axis=1).astype(jnp.int32)
    global_id = jnp.arange(DEVICES, dtype=jnp.int32)[:, None] * TILE_PLACES + slot_ids[None, :]
    at_cell = (place[:, :, None] == cell_ids[None, None, :]) & filled[:, :, None]
    grid = jnp.sum(jnp.where(at_cell, global_id[:, :, None] + 1, 0), axis=1) - 1
    grid = grid.reshape(DEVICES * RX, RY, RZ).astype(jnp.int32)
    padded = jnp.pad(grid, 1, constant_values=-1)
    stacked = jnp.stack([padded[:-2, 1:-1, 1:-1], padded[2:, 1:-1, 1:-1], padded[1:-1, :-2, 1:-1], padded[1:-1, 2:, 1:-1], padded[1:-1, 1:-1, :-2], padded[1:-1, 1:-1, 2:]])
    pos_x = jnp.arange(DEVICES, dtype=jnp.int32)[:, None] * RX + place // (RY * RZ)
    pos_y = place // RZ % RY
    pos_z = place % RZ
    found = stacked[:, pos_x, pos_y, pos_z]
    found = jnp.transpose(found, (1, 2, 0))
    neighbours = jnp.where(filled[:, :, None], found, -1).reshape(BRICKS, 6).astype(jnp.int32)
    density = jax.random.randint(keys[5], (BRICKS, 1), 1, 4)
    voxel_draw = jax.random.randint(keys[6], (BRICKS, V), 0, 5)
    occupancy = ((voxel_draw < density) & filled.reshape(BRICKS, 1)).astype(jnp.int32)
    return (send_pick, occupancy, neighbours)


def draw_send_pick(key, part):
    return brick_layout(key)[0]


def draw_occupancy(key, part):
    return brick_layout(key)[1]


def draw_neighbours(key, part):
    return brick_layout(key)[2]


def block_scale(rng, dims, cuts, smallest, largest):
    level = 1.0
    for axis_at, shards_of in cuts:
        steps = jax.random.uniform(jax.random.fold_in(jax.random.fold_in(rng, 6), axis_at), (shards_of,), jnp.float32, smallest / len(cuts), largest / len(cuts))
        level = level * jnp.repeat(jnp.exp(steps), dims[axis_at] // shards_of).reshape((-1,) + (1,) * (len(dims) - 1 - axis_at))
    return level


def bell_draw(own_key, shape, deviation, limit, shards=(), held_as=jnp.bfloat16):
    drawn = deviation * jax.random.normal(own_key, shape, jnp.float32)
    if shards:
        drawn = drawn * block_scale(own_key, shape, shards, -0.22, 0.18)
    return jnp.clip(drawn, -limit, limit).astype(held_as)


def setup_inputs(seed: int = 0) -> dict:
    seeds = jax.random.split(jax.random.key(seed), 7)
    return {
        "features": bell_draw(seeds[0], (SOURCES, C, V), 1.0, 6.0, ((0, 128),), jnp.float32),
        "send_pick": draw_send_pick(jax.random.fold_in(seeds[6], 71), 0),
        "occupancy": draw_occupancy(jax.random.fold_in(seeds[6], 71), 0),
        "neighbours": draw_neighbours(jax.random.fold_in(seeds[6], 71), 0),
        "weight_one": bell_draw(seeds[4], (3, 3, 3, C, C), (9 * C) ** -0.5, 0.25, (), jnp.float32),
        "bias_one": bell_draw(seeds[5], (C,), 0.5, 3.0, (), jnp.float32),
    }


def take_rows(source, row_index):
    gathered = jnp.take(source, jnp.maximum(row_index, 0), axis=0)
    present_rows = (row_index >= 0).reshape((-1,) + (1,) * (gathered.ndim - 1))
    return jnp.where(present_rows, gathered, jnp.zeros_like(gathered))


def pad_sides(volume, below_y, above_y, below_z, above_z):
    edge_cells = volume.shape[3]
    lower_face = take_rows(volume[:, :, :, edge_cells - 1], below_y)[:, :, :, None]
    upper_face = take_rows(volume[:, :, :, 0], above_y)[:, :, :, None]
    widened = jnp.concatenate([lower_face, volume, upper_face], axis=3)
    lower_face = take_rows(widened[:, :, :, :, edge_cells - 1], below_z)[:, :, :, :, None]
    upper_face = take_rows(widened[:, :, :, :, 0], above_z)[:, :, :, :, None]
    return jnp.concatenate([lower_face, widened, upper_face], axis=4)


def convolve(volume, weights):
    return lax.conv_general_dilated(volume, weights, (1, 1, 1), "VALID", dimension_numbers=("NCDHW", "DHWIO", "NCDHW"), precision=lax.Precision.HIGHEST)


def layer(values, neighbours, weights, shift_bias):
    bricks = values.reshape(BRICKS, C, EDGE, EDGE, EDGE)
    lower_face = take_rows(bricks[:, :, EDGE - 1], neighbours[:, 0])[:, :, None]
    upper_face = take_rows(bricks[:, :, 0], neighbours[:, 1])[:, :, None]
    volume = jnp.concatenate([lower_face, bricks, upper_face], axis=2)
    volume = pad_sides(volume, neighbours[:, 2], neighbours[:, 3], neighbours[:, 4], neighbours[:, 5])
    blocks = volume.reshape(DEVICES, TILE_PLACES, C, EDGE + 2, EDGE + 2, EDGE + 2)
    summed = lax.map(lambda block: convolve(block, weights), blocks)
    return summed.reshape(BRICKS, C, EDGE ** 3) + shift_bias[None, :, None]


def reference(features, send_pick, occupancy, neighbours, weight_one, bias_one):
    ranks = jnp.arange(DEVICES, dtype=jnp.int32)[:, None]
    slot_ids = jnp.arange(TILE_PLACES, dtype=jnp.int32)[None, :]
    target = ((slot_ids // MOST) * N_GY + ranks % N_GY) * TILE_PLACES + (ranks // N_GY) * MOST + slot_ids % MOST
    target = target.astype(jnp.int32)
    source_row = jnp.where(send_pick >= 0, ranks * SRC + send_pick, -1).astype(jnp.int32)
    source_of = jnp.zeros((BRICKS,), jnp.int32).at[target.reshape(-1)].set(source_row.reshape(-1))
    voxel_mask = occupancy.astype(jnp.float32)[:, None, :]
    inputs = take_rows(features, source_of) * voxel_mask
    return voxel_mask * jax.nn.relu(layer(inputs, neighbours, weight_one, bias_one) + inputs)
```

```python
import jax
import jax.numpy as jnp
from jax import lax
from jax.experimental import pallas as pl
from jax.experimental.pallas import tpu as pltpu
from jax.sharding import PartitionSpec as P

F32 = jnp.float32
BF16 = jnp.bfloat16
SLOTS = 32
SRC = 16
ROWS = 8 * SLOTS


def passed_along(block, axis, distance):
    devices = range(lax.axis_size(axis))
    route = [(i - distance, i) for i in devices if i - distance in devices]
    return lax.ppermute(block, axis, route)


def lane_ids(shape):
    return lax.broadcasted_iota(jnp.int32, shape, len(shape) - 1)


def split(v):
    hi = v.astype(BF16)
    return hi, (v - hi.astype(F32)).astype(BF16)


def pack_kernel(half, pick_ref, x_ref, *refs):
    out_ref, t_ref, sem = refs[-3:]
    lanes = lane_ids((32, 128))
    low = lanes < 64
    channels = slice(32 * half, 32 * half + 32)

    def one(r, carry):
        groups = []
        for g in range(4):
            p = g // 2
            a = x_ref[r, channels, p * 128 : (p + 1) * 128]
            b = x_ref[r, channels, (p + 2) * 128 : (p + 3) * 128]
            if g % 2 == 0:
                groups.append(jnp.where(low, a, pltpu.roll(b, 64, 1)))
            else:
                groups.append(jnp.where(low, pltpu.roll(a, 64, 1), b))
        t_ref[r] = jnp.concatenate(groups, axis=0).T
        return carry

    lax.fori_loop(0, SRC, one, 0, unroll=2)

    def copy(j):
        row = jnp.maximum(pick_ref[0, j], 0)
        return pltpu.make_async_copy(t_ref.at[row], out_ref.at[j], sem.at[j])

    for j in range(SLOTS):
        copy(j).start()
    for j in range(SLOTS):
        copy(j).wait()


def pack(half, send_pick, features, after):
    return pl.pallas_call(
        lambda *refs: pack_kernel(half, *refs),
        out_shape=jax.ShapeDtypeStruct((SLOTS, 128, 128), F32),
        in_specs=[
            pl.BlockSpec(memory_space=pltpu.SMEM),
            pl.BlockSpec(memory_space=pltpu.VMEM),
        ]
        + [pl.BlockSpec(memory_space=pl.ANY)] * len(after),
        out_specs=pl.BlockSpec(memory_space=pl.ANY),
        scratch_shapes=[
            pltpu.VMEM((SRC, 128, 128), F32),
            pltpu.SemaphoreType.DMA((SLOTS,)),
        ],
        name=f"pack{half}",
        cost_estimate=pl.CostEstimate(
            flops=0, bytes_accessed=6 * 2**20, transcendentals=0
        ),
    )(send_pick, features, *after)


def masked(r_ref, m_ref, row):
    at = pl.ds(row, SLOTS, stride=128)
    return r_ref[at, :] * m_ref[at, :]


def planes_kernel(r_ref, m_ref, *refs):
    up_ref, down_ref = refs[-2:]
    lanes = lane_ids((SLOTS, 128))

    def one(q, carry):
        up = jnp.zeros((SLOTS, 128), F32)
        down = jnp.zeros((SLOTS, 128), F32)
        for g in range(4):
            yz = q * 4 + g
            v0 = masked(r_ref, m_ref, yz)
            v1 = masked(r_ref, m_ref, 64 + yz)
            v0 = pltpu.roll(v0, 32 * g, 1) if g else v0
            v1 = pltpu.roll(v1, 32 * g, 1) if g else v1
            to = (g + 3) % 4
            up = jnp.where((lanes >= 32 * to) & (lanes < 32 * to + 32), v1, up)
            down = jnp.where((lanes >= 32 * g) & (lanes < 32 * g + 32), v0, down)
        up_ref[q] = up
        down_ref[q] = down
        return carry

    lax.fori_loop(0, 16, one, 0, unroll=2)


def planes(rows, mask_rows, after):
    shape = jax.ShapeDtypeStruct((16, SLOTS, 128), F32)
    vmem = pl.BlockSpec(memory_space=pltpu.VMEM)
    return pl.pallas_call(
        planes_kernel,
        out_shape=(shape, shape),
        in_specs=[vmem, vmem] + [pl.BlockSpec(memory_space=pl.ANY)] * len(after),
        out_specs=(vmem, vmem),
        name="planes",
        cost_estimate=pl.CostEstimate(
            flops=2**20, bytes_accessed=5 * 2**20, transcendentals=0
        ),
    )(rows, mask_rows, *after)


def sides(p_ref, f_hi, f_lo):
    def spread(which, sources, targets):
        blocks = [f[y, z] for f in (f_hi, f_lo) for y, z in sources]
        moved = jnp.dot(
            p_ref[which], jnp.concatenate(blocks, axis=1), preferred_element_type=F32
        )
        n = 0
        for f in (f_hi, f_lo):
            for y, z in targets:
                f[y, z] = moved[:, n * 128 : (n + 1) * 128].astype(BF16)
                n += 1

    inner = range(1, 9)
    spread(0, [(8, z) for z in inner], [(0, z) for z in inner])
    spread(1, [(1, z) for z in inner], [(9, z) for z in inner])
    spread(2, [(y, 8) for y in range(10)], [(y, 0) for y in range(10)])
    spread(3, [(y, 1) for y in range(10)], [(y, 9) for y in range(10)])


def fill_mid(i, r_ref, m_ref, f_hi, f_lo):
    lanes = lane_ids((SLOTS, 128))
    upper = lanes < 32 + 64 * i

    def one(y, carry):
        for z in range(8):
            yz = y * 8 + z
            v0 = masked(r_ref, m_ref, yz)
            v1 = masked(r_ref, m_ref, 64 + yz)
            hi, lo = split(jnp.where(upper, v1, v0))
            f_hi[y + 1, z + 1] = hi
            f_lo[y + 1, z + 1] = lo
        return carry

    lax.fori_loop(0, 8, one, 0)


def fill_ends(i, r_ref, m_ref, px_ref, low_ref, high_ref, f_hi, f_lo):
    lanes = lane_ids((SLOTS, 128))
    outer = (lanes >= 96 - 96 * i) & (lanes < 128 - 96 * i)

    def one(q, carry):
        far = jnp.where(i == 0, low_ref[q], high_ref[q])
        base, his, los = [], [], []
        for g in range(4):
            yz = q * 4 + g
            near = i * 64 + yz
            other = (1 - i) * 64 + yz
            base.append(split(masked(r_ref, m_ref, near)))
            v = masked(r_ref, m_ref, other)
            w = pltpu.roll(far, 128 - 32 * g, 1) if g else far
            v_hi, v_lo = split(v)
            w_hi, w_lo = split(w)
            his.append(jnp.concatenate([v_hi, w_hi], axis=0))
            los.append(jnp.concatenate([v_lo, w_lo], axis=0))
        moved = jnp.dot(
            px_ref[0], jnp.concatenate(his + los, axis=1), preferred_element_type=F32
        )
        for g in range(4):
            yz = q * 4 + g
            y, z = q // 2 + 1, (q % 2) * 4 + g + 1
            b_hi, b_lo = base[g]
            m_hi = moved[:, g * 128 : (g + 1) * 128]
            m_lo = moved[:, (g + 4) * 128 : (g + 5) * 128]
            f_hi[y, z] = jnp.where(outer, m_hi, b_hi.astype(F32)).astype(BF16)
            f_lo[y, z] = jnp.where(outer, m_lo, b_lo.astype(F32)).astype(BF16)
        return carry

    lax.fori_loop(0, 16, one, 0)


def convolve(f_hi, f_lo, w_ref, store):
    def one(y, carry):
        parts = []
        for j in range(3):
            for k in range(3):
                parts.append(f_hi[y + j, k : k + 8].reshape(ROWS, 128))
                parts.append(f_lo[y + j, k : k + 8].reshape(ROWS, 128))
        both = jnp.dot(
            jnp.concatenate(parts, axis=1), w_ref[0, 0], preferred_element_type=F32
        )
        store(y, both[:, :128] + both[:, 128:])
        return carry

    lax.fori_loop(0, 8, one, 0)


def finish(acc_ref, occ_ref, bias_ref, out_ref):
    low = lane_ids((64, 128)) < 64
    bias = bias_ref[...]

    def one(n, carry):
        b = 2 * n
        rows = [acc_ref[pl.ds(b + d, 64, stride=SLOTS), :] for d in range(2)]
        t = jnp.concatenate(rows, axis=0).T
        even, odd = t[:64], t[64:]
        first = jnp.where(low, even, pltpu.roll(odd, 64, 1))
        second = jnp.where(low, pltpu.roll(even, 64, 1), odd)
        for d, value in enumerate((first, second)):
            mask = occ_ref[pl.ds(b + d, 1), :].astype(F32)
            out_ref[b + d] = mask * jnp.maximum(value + bias, 0.0)
        return carry

    lax.fori_loop(0, SLOTS // 2, one, 0)


def body(mid, last, refs):
    i = pl.program_id(0)
    r_ref, m_ref, p_ref, w_ref, *refs = refs
    extra = []
    if not mid:
        extra, refs = refs[:3], refs[3:]
    if last:
        acc_in, occ_ref, bias_ref, *refs = refs
        if not mid:
            refs = refs[1:]
    out_ref, f_hi, f_lo, *refs = refs
    if mid:
        fill_mid(i, r_ref, m_ref, f_hi, f_lo)
    else:
        fill_ends(i, r_ref, m_ref, *extra, f_hi, f_lo)
    sides(p_ref, f_hi, f_lo)
    if last:
        acc_ref = refs[0]

        def store(y, value):
            at = pl.ds(pl.multiple_of(y * ROWS, ROWS), ROWS)
            acc_ref[at, :] = value + acc_in[0, at, :]

        convolve(f_hi, f_lo, w_ref, store)
        finish(acc_ref, occ_ref, bias_ref, out_ref)
    else:

        def store(y, value):
            at = pl.ds(pl.multiple_of(y * ROWS, ROWS), ROWS)
            out_ref[0, at, :] = value

        convolve(f_hi, f_lo, w_ref, store)


def stage(mid, h, rows, mask_rows, perms, weights, ends=(), before=None, final=()):
    last = before is not None
    place = (lambda i: 1 + i) if mid else (lambda i: 3 * i)
    kind = (lambda i: 1 - i) if mid else (lambda i: i)
    vmem = pl.BlockSpec(memory_space=pltpu.VMEM)
    operands = [rows, mask_rows, perms, weights]
    specs = [vmem, vmem, vmem, pl.BlockSpec((1, 1, 18 * 128, 256), lambda i: (h, kind(i), 0, 0))]
    if not mid:
        operands += list(ends)
        specs += [pl.BlockSpec((1, SLOTS, 2 * SLOTS), lambda i: (i, 0, 0)), vmem, vmem]
    scratch = [pltpu.VMEM((10, 10, SLOTS, 128), BF16)] * 2
    acc_shape = (2, 64 * SLOTS, 128)
    acc_spec = pl.BlockSpec((1,) + acc_shape[1:], lambda i: (i, 0, 0))
    aliases = {}
    if last:
        occupancy, bias, *partial = final
        operands += [before, occupancy, bias]
        specs += [acc_spec, pl.BlockSpec((SLOTS, 128), lambda i: (0, place(i))), vmem]
        if not mid:
            aliases = {len(operands): 0}
            operands += partial
            specs += [pl.BlockSpec(memory_space=pl.ANY)]
        out_shape = jax.ShapeDtypeStruct((SLOTS, 64, 512), F32)
        out_spec = pl.BlockSpec((SLOTS, 64, 128), lambda i: (0, 0, place(i)))
        scratch = scratch + [pltpu.VMEM(acc_shape[1:], F32)]
    else:
        out_shape = jax.ShapeDtypeStruct(acc_shape, F32)
        out_spec = acc_spec
    return pl.pallas_call(
        lambda *refs: body(mid, last, refs),
        out_shape=out_shape,
        grid=(2,),
        in_specs=specs,
        out_specs=out_spec,
        scratch_shapes=scratch,
        input_output_aliases=aliases,
        compiler_params=pltpu.CompilerParams(vmem_limit_bytes=48 * 2**20),
        name=("mid" if mid else "ends") + ("1" if last else "0"),
        cost_estimate=pl.CostEstimate(
            flops=2 * 2 * 2048 * 2304 * 256, bytes_accessed=8 * 2**20, transcendentals=0
        ),
    )(*operands)


def mask_kernel(occ_ref, out_ref):
    group = lax.broadcasted_iota(jnp.int32, (8, 128), 0)
    spread = (lane_ids((8, 128)) // 32 == group).astype(F32)

    def one(b, carry):
        at = pl.ds(pl.multiple_of(b * 128, 128), 128)
        out_ref[at, :] = jnp.dot(occ_ref[b].T, spread, preferred_element_type=F32)
        return carry

    lax.fori_loop(0, SLOTS, one, 0, unroll=2)


def mask_table(occupancy):
    m = occupancy.astype(F32).reshape(SLOTS, 2, 4, 64).transpose(0, 2, 1, 3)
    m = jnp.pad(m.reshape(SLOTS, 4, 128), ((0, 0), (0, 4), (0, 0)))
    return pl.pallas_call(
        mask_kernel,
        out_shape=jax.ShapeDtypeStruct((SLOTS * 128, 128), F32),
        name="masks",
        cost_estimate=pl.CostEstimate(
            flops=2**20, bytes_accessed=2 * 2**20, transcendentals=0
        ),
    )(m)


def weight_kernel(w_ref, out_ref):
    h = pl.program_id(0)
    row = lax.broadcasted_iota(jnp.int32, (32, 128), 0) + 32 * h
    lanes = lane_ids((32, 128))
    low = lanes < 64
    eye = (lanes % 64 == row).astype(F32)
    zero = jnp.zeros((32, 128), F32)
    channels = pl.ds(pl.multiple_of(32 * h, 32), 32)
    for jk in range(9):
        taps = [w_ref[9 * i + jk, channels, :] for i in range(3)]
        if jk == 4:
            taps[1] = taps[1] + eye
        taps = taps + [zero]
        window = [split(jnp.where(low, taps[d], taps[d - 1])) for d in range(4)]
        for kind, order in enumerate(((1, 2, 3, 0), (3, 0, 1, 2))):
            hi = jnp.concatenate([window[d][0] for d in order], axis=0)
            lo = jnp.concatenate([window[d][1] for d in order], axis=0)
            at = 256 * jk
            out_ref[0, kind, at : at + 128, :128] = hi
            out_ref[0, kind, at : at + 128, 128:] = lo
            out_ref[0, kind, at + 128 : at + 256, :128] = lo
            out_ref[0, kind, at + 128 : at + 256, 128:] = hi


def weight_tables(weights):
    w = weights.reshape(27, 64, 64)
    return pl.pallas_call(
        weight_kernel,
        out_shape=jax.ShapeDtypeStruct((2, 2, 18 * 128, 256), BF16),
        grid=(2,),
        in_specs=[pl.BlockSpec(memory_space=pltpu.VMEM)],
        out_specs=pl.BlockSpec((1, 2, 18 * 128, 256), lambda h: (h, 0, 0, 0)),
        name="weights",
        cost_estimate=pl.CostEstimate(
            flops=2**20, bytes_accessed=6 * 2**20, transcendentals=0
        ),
    )(jnp.concatenate([w, w], axis=2))


def owner(receive, occupancy, neighbours, own_rank, weight_one, bias_one, shift):
    mask_rows = mask_table(occupancy)
    tables = weight_tables(weight_one)
    bias = jnp.broadcast_to(bias_one[:, None], (64, 128))
    present = neighbours >= 0
    local = neighbours % SLOTS
    away = (neighbours // SLOTS != own_rank).astype(jnp.int32) * SLOTS
    ids = jnp.where(present, local, -1)
    slots = jnp.arange(SLOTS, dtype=jnp.int32)
    perms = (ids[:, 2:].T[:, :, None] == slots).astype(BF16)
    wide = jnp.where(present, local + away, -1)[:, :2]
    places = jnp.arange(2 * SLOTS, dtype=jnp.int32)
    perms_x = (wide.T[:, :, None] == places).astype(BF16)
    rows = receive(0, ()).reshape(SLOTS * 128, 128)
    later = receive(1, (mask_rows, tables)).reshape(SLOTS * 128, 128)
    up, down = planes(rows, mask_rows, ())
    ends = (perms_x, shift(up, 1), shift(down, -1))
    kept_mid = stage(True, 0, rows, mask_rows, perms, tables)
    kept_ends = stage(False, 0, rows, mask_rows, perms, tables, ends)
    up, down = planes(later, mask_rows, (kept_mid, kept_ends))
    ends = (perms_x, shift(up, 1), shift(down, -1))
    final = (occupancy, bias)
    out = stage(True, 1, later, mask_rows, perms, tables, (), kept_mid, final)
    final = (occupancy, bias, out)
    return stage(False, 1, later, mask_rows, perms, tables, ends, kept_ends, final)


def shards(features, send_pick, occupancy, neighbours, weight_one, bias_one):
    def receive(h, after):
        outgoing = pack(h, send_pick, features, after)
        return lax.all_to_all(outgoing, "gx", split_axis=0, concat_axis=0, tiled=True)

    own_rank = lax.axis_index(("gx", "gy"))
    return owner(
        receive,
        occupancy,
        neighbours,
        own_rank,
        weight_one,
        bias_one,
        lambda block, distance: passed_along(block, ("gx", "gy"), distance),
    )


def solution(mesh):
    in_specs = (
        P(("gx", "gy"), None, None),
        P(("gx", "gy"), None),
        P(("gx", "gy"), None),
        P(("gx", "gy"), None),
        P(),
        P(),
    )
    out_specs = P(("gx", "gy"), None, None)
    return jax.shard_map(shards, mesh=mesh, in_specs=in_specs, out_specs=out_specs, check_vma=False)
```

```python
import jax
import jax.numpy as jnp
from jax import lax
from jax.experimental import pallas as pl
from jax.experimental.pallas import tpu as pltpu
from jax.sharding import PartitionSpec as P

F32 = jnp.float32
BF16 = jnp.bfloat16
SLOTS = 32
SRC = 16
ROWS = 8 * SLOTS
GRANT = 67043328


def passed_along(block, axis, distance):
    devices = range(lax.axis_size(axis))
    route = [(i - distance, i) for i in devices if i - distance in devices]
    return lax.ppermute(block, axis, route)


def lane_ids(shape):
    return lax.broadcasted_iota(jnp.int32, shape, len(shape) - 1)


def split(v):
    hi = v.astype(BF16)
    return hi, (v - hi.astype(F32)).astype(BF16)


def pack_kernel(half, pick_ref, x_ref, *refs):
    out_ref, t_ref, sem = refs[-3:]
    lanes = lane_ids((32, 128))
    low = lanes < 64
    channels = slice(32 * half, 32 * half + 32)

    def one(r, carry):
        groups = []
        for g in range(4):
            p = g // 2
            a = x_ref[r, channels, p * 128 : (p + 1) * 128]
            b = x_ref[r, channels, (p + 2) * 128 : (p + 3) * 128]
            if g % 2 == 0:
                groups.append(jnp.where(low, a, pltpu.roll(b, 64, 1)))
            else:
                groups.append(jnp.where(low, pltpu.roll(a, 64, 1), b))
        t_ref[r] = jnp.concatenate(groups, axis=0).T
        return carry

    lax.fori_loop(0, SRC, one, 0, unroll=2)

    def copy(j):
        row = jnp.maximum(pick_ref[0, j], 0)
        return pltpu.make_async_copy(t_ref.at[row], out_ref.at[j], sem.at[j])

    for j in range(SLOTS):
        copy(j).start()
    for j in range(SLOTS):
        copy(j).wait()


def pack(half, send_pick, features, after):
    return pl.pallas_call(
        lambda *refs: pack_kernel(half, *refs),
        out_shape=jax.ShapeDtypeStruct((SLOTS, 128, 128), F32),
        in_specs=[
            pl.BlockSpec(memory_space=pltpu.SMEM),
            pl.BlockSpec(memory_space=pltpu.VMEM),
        ]
        + [pl.BlockSpec(memory_space=pl.ANY)] * len(after),
        out_specs=pl.BlockSpec(memory_space=pl.ANY),
        scratch_shapes=[
            pltpu.VMEM((SRC, 128, 128), F32),
            pltpu.SemaphoreType.DMA((SLOTS,)),
        ],
        name=f"pack{half}",
        compiler_params=pltpu.CompilerParams(vmem_limit_bytes=GRANT),
        cost_estimate=pl.CostEstimate(
            flops=0, bytes_accessed=6 * 2**20, transcendentals=0
        ),
    )(send_pick, features, *after)


def masked(r_ref, m_ref, at, tile):
    rows = r_ref[at, tile] * m_ref[at, tile]
    return rows.reshape(rows.shape[0] * 8, 128)


def tile_rows(v_ref, tile):
    return v_ref[:, tile].reshape(ROWS, 128)


def planes_kernel(r_ref, m_ref, *refs):
    v_ref, up_ref, down_ref = refs[-3:]
    group = lane_ids((32, 128)) // 32

    def one(c, carry):
        bricks = pl.ds(c * 4, 4)
        out = pl.ds(pl.multiple_of(c * 32, 32), 32)
        for q in range(2):
            up = jnp.zeros((32, 128), F32)
            down = jnp.zeros((32, 128), F32)
            for g in range(4):
                tile = 4 * q + g
                v0 = masked(r_ref, m_ref, bricks, tile)
                v1 = masked(r_ref, m_ref, bricks, tile + 8)
                v_ref[bricks, tile] = v0.reshape(4, 8, 128)
                v_ref[bricks, tile + 8] = v1.reshape(4, 8, 128)
                v0 = pltpu.roll(v0, 32 * g, 1) if g else v0
                v1 = pltpu.roll(v1, 32 * g, 1) if g else v1
                up = jnp.where(group == (g + 3) % 4, v1, up)
                down = jnp.where(group == g, v0, down)
            up_ref[q, out, :] = up
            down_ref[q, out, :] = down
        return carry

    lax.fori_loop(0, 2, one, 0, unroll=2)


def planes(rows, mask_rows, after):
    shape = jax.ShapeDtypeStruct((2, ROWS, 128), F32)
    brick = pl.BlockSpec((8, 16, 8, 128), lambda n: (n, 0, 0, 0))
    plane = pl.BlockSpec((2, 64, 128), lambda n: (0, n, 0))
    return pl.pallas_call(
        planes_kernel,
        out_shape=(jax.ShapeDtypeStruct((SLOTS, 16, 8, 128), F32), shape, shape),
        grid=(4,),
        in_specs=[brick, brick] + [pl.BlockSpec(memory_space=pl.ANY)] * len(after),
        out_specs=(brick, plane, plane),
        name="planes",
        compiler_params=pltpu.CompilerParams(vmem_limit_bytes=GRANT),
        cost_estimate=pl.CostEstimate(
            flops=2**20, bytes_accessed=7 * 2**20, transcendentals=0
        ),
    )(rows, mask_rows, *after)


def order_tables(order_ref):
    row = lax.broadcasted_iota(jnp.int32, (ROWS, ROWS), 0)
    column = lane_ids((ROWS, ROWS))
    forth = (((row & 31) << 3) | (row >> 5)) == column
    back = (((row & 7) << 5) | (row >> 3)) == column
    order_ref[0] = forth.astype(F32).astype(BF16)
    order_ref[1] = back.astype(F32).astype(BF16)


def moved_rows(order, value):
    both = jnp.concatenate(split(value), axis=1)
    return jnp.dot(order, both, preferred_element_type=F32)


def sides(p_ref, f_hi, f_lo):
    def spread(which, sources, targets):
        blocks = [f[y, z] for f in (f_hi, f_lo) for y, z in sources]
        moved = jnp.dot(
            p_ref[which], jnp.concatenate(blocks, axis=1), preferred_element_type=F32
        )
        n = 0
        for f in (f_hi, f_lo):
            for y, z in targets:
                f[y, z] = moved[:, n * 128 : (n + 1) * 128].astype(BF16)
                n += 1

    inner = range(1, 9)
    spread(0, [(8, z) for z in inner], [(0, z) for z in inner])
    spread(1, [(1, z) for z in inner], [(9, z) for z in inner])
    spread(2, [(y, 8) for y in range(10)], [(y, 0) for y in range(10)])
    spread(3, [(y, 1) for y in range(10)], [(y, 9) for y in range(10)])


def put(f_hi, f_lo, y, hi, lo):
    f_hi[y + 1, 1:9] = hi.astype(BF16).reshape(8, SLOTS, 128)
    f_lo[y + 1, 1:9] = lo.astype(BF16).reshape(8, SLOTS, 128)


def fill_mid(i, v_ref, order_ref, f_hi, f_lo):
    upper = lane_ids((ROWS, 128)) < 32 + 64 * i

    def one(y, carry):
        v0 = tile_rows(v_ref, y)
        v1 = tile_rows(v_ref, 8 + y)
        moved = moved_rows(order_ref[0], jnp.where(upper, v1, v0))
        put(f_hi, f_lo, y, moved[:, :128], moved[:, 128:])
        return carry

    lax.fori_loop(0, 8, one, 0, unroll=FILL_U)


def fill_ends(i, v_ref, px_ref, up, down, low, high, order_ref, halo, f_hi, f_lo):
    outer = lane_ids((ROWS, 128)) // 32 == 3 - 3 * i
    for q in range(2):
        near = jnp.where(i == 0, up[q], down[q])
        far = jnp.where(i == 0, low[q], high[q])
        halo[q] = moved_rows(px_ref[0], jnp.concatenate([near, far], axis=0))

    def one(q, carry):
        for g in range(4):
            y = q * 4 + g
            moved = moved_rows(order_ref[0], tile_rows(v_ref, 8 * i + y))
            parts = []
            for part in range(2):
                side = halo[q, :, 128 * part : 128 * part + 128]
                side = pltpu.roll(side, 128 - 32 * g, 1) if g else side
                parts.append(
                    jnp.where(outer, side, moved[:, 128 * part : 128 * part + 128])
                )
            put(f_hi, f_lo, y, *parts)
        return carry

    lax.fori_loop(0, 2, one, 0, unroll=2)


CONV_Y = 2
CONV_U = 4
FILL_U = 8


def convolve(f_hi, f_lo, w_ref, store):
    def one(t, carry):
        parts = []
        for j in range(3):
            for k in range(3):
                for f in (f_hi, f_lo):
                    rows = f[pl.ds(t * CONV_Y + j, CONV_Y), k : k + 8]
                    parts.append(rows.reshape(CONV_Y * ROWS, 128))
        both = jnp.dot(
            jnp.concatenate(parts, axis=1), w_ref[0, 0], preferred_element_type=F32
        )
        for d in range(CONV_Y):
            at = slice(d * ROWS, (d + 1) * ROWS)
            store(t * CONV_Y + d, both[at, :128] + both[at, 128:])
        return carry

    lax.fori_loop(0, 8 // CONV_Y, one, 0, unroll=CONV_U)


def by_brick(order_ref, sum_ref, acc_ref):
    for y in range(8):
        back = moved_rows(order_ref[1], sum_ref[y * ROWS : (y + 1) * ROWS, :])
        acc_ref[:, y] = (back[:, :128] + back[:, 128:]).reshape(SLOTS, 8, 128)


def finish(acc_ref, occ_ref, bias_ref, out_ref):
    low = lane_ids((64, 128)) < 64
    bias = bias_ref[...]

    def one(n, carry):
        b = 2 * n
        rows = acc_ref[pl.ds(b, 2)].reshape(128, 128)
        t = rows.T
        even, odd = t[:64], t[64:]
        first = jnp.where(low, even, pltpu.roll(odd, 64, 1))
        second = jnp.where(low, pltpu.roll(even, 64, 1), odd)
        for d, value in enumerate((first, second)):
            mask = occ_ref[pl.ds(b + d, 1), :].astype(F32)
            out_ref[b + d] = mask * jnp.maximum(value + bias, 0.0)
        return carry

    lax.fori_loop(0, SLOTS // 2, one, 0, unroll=4)


def body(mid, last, refs):
    i = pl.program_id(0)
    v_ref, p_ref, w_ref, *refs = refs
    extra = []
    if not mid:
        extra, refs = refs[:5], refs[5:]
    if last:
        acc_in, occ_ref, bias_ref, *refs = refs
        if not mid:
            refs = refs[1:]
    out_ref, f_hi, f_lo, order_ref, halo, *refs = refs

    @pl.when(i == 0)
    def _():
        order_tables(order_ref)

    if mid:
        fill_mid(i, v_ref, order_ref, f_hi, f_lo)
    else:
        fill_ends(i, v_ref, *extra, order_ref, halo, f_hi, f_lo)
    sides(p_ref, f_hi, f_lo)
    if last:
        sum_ref, acc_ref = refs

        def store(y, value):
            at = pl.ds(pl.multiple_of(y * ROWS, ROWS), ROWS)
            sum_ref[at, :] = value + acc_in[0, at, :]

        convolve(f_hi, f_lo, w_ref, store)
        by_brick(order_ref, sum_ref, acc_ref)
        finish(acc_ref, occ_ref, bias_ref, out_ref)
    else:

        def store(y, value):
            at = pl.ds(pl.multiple_of(y * ROWS, ROWS), ROWS)
            out_ref[0, at, :] = value

        convolve(f_hi, f_lo, w_ref, store)


def stage(mid, h, rows, perms, weights, ends=(), before=None, final=()):
    last = before is not None
    place = (lambda i: 1 + i) if mid else (lambda i: 3 * i)
    kind = (lambda i: 1 - i) if mid else (lambda i: i)
    vmem = pl.BlockSpec(memory_space=pltpu.VMEM)
    operands = [rows, perms, weights]
    specs = [vmem, vmem, pl.BlockSpec((1, 1, 18 * 128, 256), lambda i: (h, kind(i), 0, 0))]
    if not mid:
        operands += list(ends)
        specs += [pl.BlockSpec((1, ROWS, 2 * ROWS), lambda i: (i, 0, 0))] + [vmem] * 4
    scratch = [pltpu.VMEM((10, 10, SLOTS, 128), BF16)] * 2
    scratch += [pltpu.VMEM((2, ROWS, ROWS), BF16), pltpu.VMEM((2, ROWS, ROWS), F32)]
    acc_shape = (2, 64 * SLOTS, 128)
    acc_spec = pl.BlockSpec((1,) + acc_shape[1:], lambda i: (i, 0, 0))
    aliases = {}
    if last:
        occupancy, bias, *partial = final
        operands += [before, occupancy, bias]
        specs += [acc_spec, pl.BlockSpec((SLOTS, 128), lambda i: (0, place(i))), vmem]
        if not mid:
            aliases = {len(operands): 0}
            operands += partial
            specs += [pl.BlockSpec(memory_space=pl.ANY)]
        out_shape = jax.ShapeDtypeStruct((SLOTS, 64, 512), F32)
        out_spec = pl.BlockSpec((SLOTS, 64, 128), lambda i: (0, 0, place(i)))
        scratch += [pltpu.VMEM(acc_shape[1:], F32), pltpu.VMEM((SLOTS, 8, 8, 128), F32)]
    else:
        out_shape = jax.ShapeDtypeStruct(acc_shape, F32)
        out_spec = acc_spec
    return pl.pallas_call(
        lambda *refs: body(mid, last, refs),
        out_shape=out_shape,
        grid=(2,),
        in_specs=specs,
        out_specs=out_spec,
        scratch_shapes=scratch,
        input_output_aliases=aliases,
        compiler_params=pltpu.CompilerParams(vmem_limit_bytes=GRANT),
        name=("mid" if mid else "ends") + ("1" if last else "0"),
        cost_estimate=pl.CostEstimate(
            flops=2 * 2 * 2048 * 2304 * 256, bytes_accessed=8 * 2**20, transcendentals=0
        ),
    )(*operands)


def mask_kernel(occ_ref, out_ref):
    group = lax.broadcasted_iota(jnp.int32, (8, 128), 0)
    spread = (lane_ids((8, 128)) // 32 == group).astype(F32)

    def one(b, carry):
        at = pl.ds(pl.multiple_of(b * 128, 128), 128)
        out_ref[at, :] = jnp.dot(occ_ref[b].T, spread, preferred_element_type=F32)
        return carry

    lax.fori_loop(0, SLOTS, one, 0, unroll=2)


def mask_table(occupancy):
    m = occupancy.astype(F32).reshape(SLOTS, 2, 4, 64).transpose(0, 2, 1, 3)
    m = jnp.pad(m.reshape(SLOTS, 4, 128), ((0, 0), (0, 4), (0, 0)))
    return pl.pallas_call(
        mask_kernel,
        out_shape=jax.ShapeDtypeStruct((SLOTS * 128, 128), F32),
        name="masks",
        compiler_params=pltpu.CompilerParams(vmem_limit_bytes=GRANT),
        cost_estimate=pl.CostEstimate(
            flops=2**20, bytes_accessed=2 * 2**20, transcendentals=0
        ),
    )(m)


def weight_kernel(w_ref, out_ref):
    h = pl.program_id(0)
    row = lax.broadcasted_iota(jnp.int32, (32, 128), 0) + 32 * h
    lanes = lane_ids((32, 128))
    low = lanes < 64
    eye = (lanes % 64 == row).astype(F32)
    zero = jnp.zeros((32, 128), F32)
    channels = pl.ds(pl.multiple_of(32 * h, 32), 32)
    for jk in range(9):
        taps = [w_ref[9 * i + jk, channels, :] for i in range(3)]
        if jk == 4:
            taps[1] = taps[1] + eye
        taps = taps + [zero]
        window = [split(jnp.where(low, taps[d], taps[d - 1])) for d in range(4)]
        for kind, order in enumerate(((1, 2, 3, 0), (3, 0, 1, 2))):
            hi = jnp.concatenate([window[d][0] for d in order], axis=0)
            lo = jnp.concatenate([window[d][1] for d in order], axis=0)
            at = 256 * jk
            out_ref[0, kind, at : at + 128, :128] = hi
            out_ref[0, kind, at : at + 128, 128:] = lo
            out_ref[0, kind, at + 128 : at + 256, :128] = lo
            out_ref[0, kind, at + 128 : at + 256, 128:] = hi


def weight_tables(weights):
    w = weights.reshape(27, 64, 64)
    return pl.pallas_call(
        weight_kernel,
        out_shape=jax.ShapeDtypeStruct((2, 2, 18 * 128, 256), BF16),
        grid=(2,),
        in_specs=[pl.BlockSpec(memory_space=pltpu.VMEM)],
        out_specs=pl.BlockSpec((1, 2, 18 * 128, 256), lambda h: (h, 0, 0, 0)),
        name="weights",
        compiler_params=pltpu.CompilerParams(vmem_limit_bytes=GRANT),
        cost_estimate=pl.CostEstimate(
            flops=2**20, bytes_accessed=6 * 2**20, transcendentals=0
        ),
    )(jnp.concatenate([w, w], axis=2))


def owner(receive, occupancy, neighbours, own_rank, weight_one, bias_one, shift):
    mask_rows = mask_table(occupancy).reshape(SLOTS, 16, 8, 128)
    tables = weight_tables(weight_one)
    bias = jnp.broadcast_to(bias_one[:, None], (64, 128))
    present = neighbours >= 0
    local = neighbours % SLOTS
    away = (neighbours // SLOTS != own_rank).astype(jnp.int32) * SLOTS
    ids = jnp.where(present, local, -1)
    slots = jnp.arange(SLOTS, dtype=jnp.int32)
    perms = (ids[:, 2:].T[:, :, None] == slots).astype(BF16)
    wide = jnp.where(present, local + away, -SLOTS * 8)[:, :2].T[:, None, :] * 8
    wide = wide + jnp.arange(8, dtype=jnp.int32)[:, None]
    places = jnp.arange(2 * ROWS, dtype=jnp.int32)
    perms_x = (wide.reshape(2, ROWS)[:, :, None] == places).astype(BF16)
    rows = receive(0, ()).reshape(SLOTS, 16, 8, 128)
    later = receive(1, (mask_rows, tables, perms, perms_x)).reshape(SLOTS, 16, 8, 128)
    rows, up, down = planes(rows, mask_rows, ())
    ends = (perms_x, up, down, shift(up, 1), shift(down, -1))
    kept_mid = stage(True, 0, rows, perms, tables)
    kept_ends = stage(False, 0, rows, perms, tables, ends)
    rows, up, down = planes(later, mask_rows, (kept_mid, kept_ends))
    ends = (perms_x, up, down, shift(up, 1), shift(down, -1))
    final = (occupancy, bias)
    out = stage(True, 1, rows, perms, tables, (), kept_mid, final)
    final = (occupancy, bias, out)
    return stage(False, 1, rows, perms, tables, ends, kept_ends, final)


def shards(features, send_pick, occupancy, neighbours, weight_one, bias_one):
    def receive(h, after):
        outgoing = pack(h, send_pick, features, after)
        return lax.all_to_all(outgoing, "gx", split_axis=0, concat_axis=0, tiled=True)

    own_rank = lax.axis_index(("gx", "gy"))
    return owner(
        receive,
        occupancy,
        neighbours,
        own_rank,
        weight_one,
        bias_one,
        lambda block, distance: passed_along(block, ("gx", "gy"), distance),
    )


def solution(mesh):
    in_specs = (
        P(("gx", "gy"), None, None),
        P(("gx", "gy"), None),
        P(("gx", "gy"), None),
        P(("gx", "gy"), None),
        P(),
        P(),
    )
    out_specs = P(("gx", "gy"), None, None)
    return jax.shard_map(shards, mesh=mesh, in_specs=in_specs, out_specs=out_specs, check_vma=False)
```

```python
import jax
import jax.numpy as jnp
from jax import lax
from jax.experimental import pallas as pl
from jax.experimental.pallas import tpu as pltpu
from jax.sharding import PartitionSpec as P

F32 = jnp.float32
BF16 = jnp.bfloat16
SLOTS = 32
SRC = 16
ROWS = 8 * SLOTS
GRANT = 67043328


def passed_along(block, axis, distance):
    devices = range(lax.axis_size(axis))
    route = [(i - distance, i) for i in devices if i - distance in devices]
    return lax.ppermute(block, axis, route)


def lane_ids(shape):
    return lax.broadcasted_iota(jnp.int32, shape, len(shape) - 1)


def split(v):
    hi = v.astype(BF16)
    return hi, (v - hi.astype(F32)).astype(BF16)


def turned(x_ref, r, channels):
    low = lane_ids((32, 128)) < 64
    groups = []
    for g in range(4):
        p = g // 2
        a = x_ref[r, channels, p * 128 : (p + 1) * 128]
        b = x_ref[r, channels, (p + 2) * 128 : (p + 3) * 128]
        if g % 2 == 0:
            groups.append(jnp.where(low, a, pltpu.roll(b, 64, 1)))
        else:
            groups.append(jnp.where(low, pltpu.roll(a, 64, 1), b))
    return jnp.concatenate(groups, axis=0).T


def pack_first(x_ref, t_ref):
    channels = slice(32, 64)
    low = lane_ids((32, 128)) < 64
    group = lane_ids((8, 128)) // 32
    both = []
    for r in range(4):
        t_ref[r, :128] = turned(x_ref, r, slice(0, 32))
        both.append(jnp.where(low, x_ref[r, channels, :128], x_ref[r, channels, 384:]))
    planes_t = jnp.concatenate(both, axis=0).T
    for r in range(4):
        for plane in range(2):
            for q in range(2):
                value = None
                for g in range(4):
                    at = (1 - plane) * 64 + (4 * q + g) * 8
                    to = (g + 3) % 4 if plane == 0 else g
                    tile = planes_t[at : at + 8]
                    if to != r:
                        tile = pltpu.roll(tile, (32 * (to - r)) % 128, 1)
                    value = tile if value is None else jnp.where(group == to, tile, value)
                at = 128 + (2 * plane + q) * 8
                t_ref[r, at : at + 8] = value


def pack_second(x_ref, t_ref):
    group = lane_ids((64, 128)) // 32
    group_b = lane_ids((32, 128)) // 32
    inner = (group_b == 1) | (group_b == 2)
    for r in range(4):
        t = turned(x_ref, r, slice(32, 64))
        t_ref[r, :64] = jnp.where(group == 0, t[64:], t[:64])
        t_ref[r, 64:96] = jnp.where(inner, t[64:96], pltpu.roll(t[96:], 64, 1))


def pack_kernel(half, pick_ref, x_ref, *refs):
    out_ref, t_ref, slot_ref, sem = refs[-4:]
    n = pl.program_id(0)

    @pl.when(n == 0)
    def _():
        for j in range(SLOTS):
            p = pick_ref[0, j]
            slot_ref[jnp.where(p < 0, SRC, p)] = j

    (pack_second if half else pack_first)(x_ref, t_ref.at[pl.ds(4 * n, 4)])

    def copy(r):
        return pltpu.make_async_copy(t_ref.at[r], out_ref.at[slot_ref[r]], sem.at[r])

    for r in range(4):
        copy(4 * n + r).start()

    @pl.when(n == 3)
    def _():
        for r in range(SRC):
            copy(r).wait()


def pack(half, send_pick, features, after):
    rows = 96 if half else 160
    return pl.pallas_call(
        lambda *refs: pack_kernel(half, *refs),
        out_shape=jax.ShapeDtypeStruct((SLOTS, rows, 128), F32),
        grid=(4,),
        in_specs=[
            pl.BlockSpec(memory_space=pltpu.SMEM),
            pl.BlockSpec((4, 64, 512), lambda n: (n, 0, 0)),
        ]
        + [pl.BlockSpec(memory_space=pl.ANY)] * len(after),
        out_specs=pl.BlockSpec(memory_space=pl.ANY),
        scratch_shapes=[
            pltpu.VMEM((SRC, rows, 128), F32),
            pltpu.SMEM((SLOTS,), jnp.int32),
            pltpu.SemaphoreType.DMA((SRC,)),
        ],
        name=f"pack{half}",
        compiler_params=pltpu.CompilerParams(vmem_limit_bytes=GRANT),
        cost_estimate=pl.CostEstimate(
            flops=0, bytes_accessed=6 * 2**20, transcendentals=0
        ),
    )(send_pick, features, *after)


def masked(r_ref, m_ref, at, tile):
    rows = jnp.where(m_ref[at, tile] > 0, r_ref[at, tile], 0.0)
    return rows.reshape(rows.shape[0] * 8, 128)


def tile_rows(v_ref, tile):
    return v_ref[:, tile].reshape(ROWS, 128)


def planes_kernel(r_ref, m_ref, v_ref, up_ref, down_ref):
    group = lane_ids((32, 128)) // 32

    for c in range(2):
        bricks = slice(c * 4, c * 4 + 4)
        out = slice(c * 32, c * 32 + 32)
        for q in range(2):
            up = jnp.zeros((32, 128), F32)
            down = jnp.zeros((32, 128), F32)
            for g in range(4):
                tile = 4 * q + g
                v0 = masked(r_ref, m_ref, bricks, tile)
                v1 = masked(r_ref, m_ref, bricks, tile + 8)
                v_ref[bricks, tile] = v0.reshape(4, 8, 128)
                v_ref[bricks, tile + 8] = v1.reshape(4, 8, 128)
                v0 = pltpu.roll(v0, 32 * g, 1) if g else v0
                v1 = pltpu.roll(v1, 32 * g, 1) if g else v1
                up = jnp.where(group == (g + 3) % 4, v1, up)
                down = jnp.where(group == g, v0, down)
            up_ref[0, q, out, :] = up
            down_ref[0, q, out, :] = down
            up_ref[1, q, out, :] = masked(r_ref, m_ref, bricks, 16 + q)
            down_ref[1, q, out, :] = masked(r_ref, m_ref, bricks, 18 + q)


def planes(rows, mask_rows):
    shape = jax.ShapeDtypeStruct((2, 2, ROWS, 128), F32)
    tiles = pl.BlockSpec((8, 20, 8, 128), lambda n: (n, 0, 0, 0))
    brick = pl.BlockSpec((8, 16, 8, 128), lambda n: (n, 0, 0, 0))
    plane = pl.BlockSpec((2, 2, 64, 128), lambda n: (0, 0, n, 0))
    return pl.pallas_call(
        planes_kernel,
        out_shape=(jax.ShapeDtypeStruct((SLOTS, 16, 8, 128), F32), shape, shape),
        grid=(4,),
        in_specs=[tiles, tiles],
        out_specs=(brick, plane, plane),
        name="planes",
        compiler_params=pltpu.CompilerParams(vmem_limit_bytes=GRANT),
        cost_estimate=pl.CostEstimate(
            flops=2**20, bytes_accessed=8 * 2**20, transcendentals=0
        ),
    )(rows, mask_rows)


def order_tables(order_ref):
    row = lax.broadcasted_iota(jnp.int32, (ROWS, ROWS), 0)
    column = lane_ids((ROWS, ROWS))
    forth = (((row & 31) << 3) | (row >> 5)) == column
    back = (((row & 7) << 5) | (row >> 3)) == column
    order_ref[0] = forth.astype(F32).astype(BF16)
    order_ref[1] = back.astype(F32).astype(BF16)


def moved_rows(order, value):
    both = jnp.concatenate(split(value), axis=1)
    return jnp.dot(order, both, preferred_element_type=F32)


def sides(p_ref, f_hi, f_lo):
    def spread(which, sources, targets):
        blocks = [f[y, z] for f in (f_hi, f_lo) for y, z in sources]
        moved = jnp.dot(
            p_ref[which], jnp.concatenate(blocks, axis=1), preferred_element_type=F32
        )
        n = 0
        for f in (f_hi, f_lo):
            for y, z in targets:
                f[y, z] = moved[:, n * 128 : (n + 1) * 128].astype(BF16)
                n += 1

    inner = range(1, 9)
    spread(0, [(8, z) for z in inner], [(0, z) for z in inner])
    spread(1, [(1, z) for z in inner], [(9, z) for z in inner])
    spread(2, [(y, 8) for y in range(10)], [(y, 0) for y in range(10)])
    spread(3, [(y, 1) for y in range(10)], [(y, 9) for y in range(10)])


def put(f_hi, f_lo, y, hi, lo):
    f_hi[y + 1, 1:9] = hi.astype(BF16).reshape(8, SLOTS, 128)
    f_lo[y + 1, 1:9] = lo.astype(BF16).reshape(8, SLOTS, 128)


def fill_mid(i, v_ref, order_ref, f_hi, f_lo):
    upper = lane_ids((ROWS, 128)) < 32 + 64 * i

    def one(y, carry):
        v0 = tile_rows(v_ref, y)
        v1 = tile_rows(v_ref, 8 + y)
        moved = moved_rows(order_ref[0], jnp.where(upper, v1, v0))
        put(f_hi, f_lo, y, moved[:, :128], moved[:, 128:])
        return carry

    lax.fori_loop(0, 8, one, 0, unroll=FILL_U)


def fill_ends(i, v_ref, px_ref, up, down, low, high, order_ref, halo, f_hi, f_lo):
    outer = lane_ids((ROWS, 128)) // 32 == 3 - 3 * i
    for q in range(2):
        near = jnp.where(i == 0, up[0, q], down[0, q])
        far = jnp.where(i == 0, low[0, q], high[0, q])
        halo[q] = moved_rows(px_ref[0], jnp.concatenate([near, far], axis=0))

    def one(q, carry):
        for g in range(4):
            y = q * 4 + g
            moved = moved_rows(order_ref[0], tile_rows(v_ref, 8 * i + y))
            parts = []
            for part in range(2):
                side = halo[q, :, 128 * part : 128 * part + 128]
                side = pltpu.roll(side, 128 - 32 * g, 1) if g else side
                parts.append(
                    jnp.where(outer, side, moved[:, 128 * part : 128 * part + 128])
                )
            put(f_hi, f_lo, y, *parts)
        return carry

    lax.fori_loop(0, 2, one, 0, unroll=2)


def inner_rows(m, y, r_ref, m_ref):
    group = lane_ids((ROWS, 128)) // 32
    every = slice(None)
    a = masked(r_ref, m_ref, every, y)
    b = masked(r_ref, m_ref, every, 8 + y % 4)
    b = pltpu.roll(b, 64, 1) if y > 3 else b
    return jnp.where((m >= 2) & ((group == 1) | (group == 2)), b, a)


def fill_inner(m, r_ref, m_ref, order_ref, f_hi, f_lo):
    for y in range(8):
        moved = moved_rows(order_ref[0], inner_rows(m, y, r_ref, m_ref))
        put(f_hi, f_lo, y, moved[:, :128], moved[:, 128:])


def fill_outer(m, r_ref, m_ref, px_ref, up, down, low, high, order_ref, halo, f_hi, f_lo):
    group = lane_ids((ROWS, 128)) // 32
    outer = group == jnp.where(m == 0, 3, 0)
    edge = group == jnp.where(m == 0, 0, 3)
    for q in range(2):
        own = jnp.where(m == 0, down[0, q], up[0, q])
        near = jnp.where(m == 0, up[0, q], down[0, q])
        far = jnp.where(m == 0, low[0, q], high[0, q])
        halo[q] = moved_rows(px_ref[0], jnp.concatenate([near, far], axis=0))
        halo[2 + q] = moved_rows(order_ref[0], own)
    for y in range(8):
        q, g = y // 4, y % 4
        moved = moved_rows(order_ref[0], inner_rows(m, y, r_ref, m_ref))
        parts = []
        for part in range(2):
            lanes = slice(128 * part, 128 * part + 128)
            side, own = halo[q, :, lanes], halo[2 + q, :, lanes]
            if g:
                side = pltpu.roll(side, 128 - 32 * g, 1)
                own = pltpu.roll(own, 128 - 32 * g, 1)
            value = jnp.where(outer, side, moved[:, lanes])
            parts.append(jnp.where(edge, own, value))
        put(f_hi, f_lo, y, *parts)


CONV_Y = 2
CONV_U = 4
FILL_U = 8


def convolve(f_hi, f_lo, w_ref, store):
    def one(t, carry):
        parts = []
        for j in range(3):
            for k in range(3):
                for f in (f_hi, f_lo):
                    rows = f[pl.ds(t * CONV_Y + j, CONV_Y), k : k + 8]
                    parts.append(rows.reshape(CONV_Y * ROWS, 128))
        both = jnp.dot(
            jnp.concatenate(parts, axis=1), w_ref[0, 0], preferred_element_type=F32
        )
        for d in range(CONV_Y):
            at = slice(d * ROWS, (d + 1) * ROWS)
            store(t * CONV_Y + d, both[at, :128] + both[at, 128:])
        return carry

    lax.fori_loop(0, 8 // CONV_Y, one, 0, unroll=CONV_U)


def by_brick(order_ref, sum_ref, acc_ref):
    for y in range(8):
        back = moved_rows(order_ref[1], sum_ref[y * ROWS : (y + 1) * ROWS, :])
        acc_ref[:, y] = (back[:, :128] + back[:, 128:]).reshape(SLOTS, 8, 128)


def finish(acc_ref, occ_ref, bias_ref, out_ref):
    low = lane_ids((64, 128)) < 64
    bias = bias_ref[...]

    def one(n, carry):
        b = 2 * n
        rows = acc_ref[pl.ds(b, 2)].reshape(128, 128)
        t = rows.T
        even, odd = t[:64], t[64:]
        first = jnp.where(low, even, pltpu.roll(odd, 64, 1))
        second = jnp.where(low, pltpu.roll(even, 64, 1), odd)
        for d, value in enumerate((first, second)):
            mask = occ_ref[pl.ds(b + d, 1), :].astype(F32)
            out_ref[b + d] = mask * jnp.maximum(value + bias, 0.0)
        return carry

    lax.fori_loop(0, SLOTS // 2, one, 0, unroll=4)


def early_body(mid, refs):
    i = pl.program_id(0)
    v_ref, p_ref, w_ref, *refs = refs
    extra = []
    if not mid:
        extra, refs = refs[:5], refs[5:]
    out_ref, f_hi, f_lo, order_ref, halo = refs

    @pl.when(i == 0)
    def _():
        order_tables(order_ref)

    if mid:
        fill_mid(i, v_ref, order_ref, f_hi, f_lo)
    else:
        fill_ends(i, v_ref, *extra, order_ref, halo, f_hi, f_lo)
    sides(p_ref, f_hi, f_lo)

    def store(y, value):
        at = pl.ds(pl.multiple_of(y * ROWS, ROWS), ROWS)
        out_ref[0, at, :] = value

    convolve(f_hi, f_lo, w_ref, store)


def late_body(*refs):
    r_ref, m_ref, p_ref, w_ref, *refs = refs
    sides_refs, refs = refs[:5], refs[5:]
    acc_mid, acc_ends, occ_ref, bias_ref, out_ref, *refs = refs
    f_hi, f_lo, order_ref, halo, sum_ref, acc_ref = refs
    m = pl.program_id(0)
    mid = (m == 1) | (m == 2)

    @pl.when(m == 0)
    def _():
        order_tables(order_ref)

    @pl.when(mid)
    def _():
        fill_inner(m, r_ref, m_ref, order_ref, f_hi, f_lo)

    @pl.when(jnp.logical_not(mid))
    def _():
        fill_outer(m, r_ref, m_ref, *sides_refs, order_ref, halo, f_hi, f_lo)

    sides(p_ref, f_hi, f_lo)

    def store(y, value):
        at = pl.ds(pl.multiple_of(y * ROWS, ROWS), ROWS)
        sum_ref[at, :] = value + jnp.where(mid, acc_mid[0, at, :], acc_ends[0, at, :])

    convolve(f_hi, f_lo, w_ref, store)
    by_brick(order_ref, sum_ref, acc_ref)
    finish(acc_ref, occ_ref, bias_ref, out_ref)


VMEM = pl.BlockSpec(memory_space=pltpu.VMEM)
FIELDS = [pltpu.VMEM((10, 10, SLOTS, 128), BF16)] * 2 + [pltpu.VMEM((2, ROWS, ROWS), BF16)]
PARAMS = pltpu.CompilerParams(vmem_limit_bytes=GRANT)


def half_of(h):
    return pl.BlockSpec((1, 2, ROWS, 128), lambda i: (h, 0, 0, 0))


def early(mid, rows, perms, weights, ends=()):
    kind = (lambda i: 1 - i) if mid else (lambda i: i)
    operands = [rows, perms, weights]
    specs = [VMEM, VMEM, pl.BlockSpec((1, 1, 18 * 128, 256), lambda i: (0, kind(i), 0, 0))]
    if not mid:
        operands += list(ends)
        specs += [pl.BlockSpec((1, ROWS, 2 * ROWS), lambda i: (i, 0, 0))] + [half_of(0)] * 4
    return pl.pallas_call(
        lambda *refs: early_body(mid, refs),
        out_shape=jax.ShapeDtypeStruct((2, 64 * SLOTS, 128), F32),
        grid=(2,),
        in_specs=specs,
        out_specs=pl.BlockSpec((1, 64 * SLOTS, 128), lambda i: (i, 0, 0)),
        scratch_shapes=FIELDS + [pltpu.VMEM((2, ROWS, ROWS), F32)],
        compiler_params=PARAMS,
        name="mid" if mid else "ends",
        cost_estimate=pl.CostEstimate(
            flops=2 * 2 * 2048 * 2304 * 256, bytes_accessed=8 * 2**20, transcendentals=0
        ),
    )(*operands)


def late(rows, mask_rows, perms, weights, ends, kept_mid, kept_ends, occupancy, bias):
    acc = (1, 64 * SLOTS, 128)
    specs = [VMEM, VMEM, VMEM]
    specs += [pl.BlockSpec((1, 1, 18 * 128, 256), lambda m: (1, m % 2, 0, 0))]
    specs += [pl.BlockSpec((1, ROWS, 2 * ROWS), lambda m: (m // 2, 0, 0))] + [half_of(1)] * 4
    specs += [pl.BlockSpec(acc, lambda m: (m // 2, 0, 0))]
    specs += [pl.BlockSpec(acc, lambda m: (m // 3, 0, 0))]
    specs += [pl.BlockSpec((SLOTS, 128), lambda m: (0, m)), VMEM]
    return pl.pallas_call(
        late_body,
        out_shape=jax.ShapeDtypeStruct((SLOTS, 64, 512), F32),
        grid=(4,),
        in_specs=specs,
        out_specs=pl.BlockSpec((SLOTS, 64, 128), lambda m: (0, 0, m)),
        scratch_shapes=FIELDS
        + [
            pltpu.VMEM((4, ROWS, ROWS), F32),
            pltpu.VMEM(acc[1:], F32),
            pltpu.VMEM((SLOTS, 8, 8, 128), F32),
        ],
        compiler_params=PARAMS,
        name="late",
        cost_estimate=pl.CostEstimate(
            flops=4 * 2 * 2048 * 2304 * 256, bytes_accessed=16 * 2**20, transcendentals=0
        ),
    )(rows, mask_rows, perms, weights, *ends, kept_mid, kept_ends, occupancy, bias)


def mask_kernel(occ_ref, first_ref, second_ref):
    group = lax.broadcasted_iota(jnp.int32, (8, 128), 0)
    spread = (lane_ids((8, 128)) // 32 == group).astype(F32)

    def one(b, carry):
        rows = jnp.dot(occ_ref[b].T, spread, preferred_element_type=F32)
        first_ref[b] = rows[:160].reshape(20, 8, 128)
        second_ref[b] = rows[160:].reshape(12, 8, 128)
        return carry

    lax.fori_loop(0, SLOTS, one, 0, unroll=2)


def mask_tables(occupancy):
    occ = occupancy.astype(F32).reshape(SLOTS, 8, 64)
    base = occ.reshape(SLOTS, 2, 4, 64).transpose(0, 2, 1, 3).reshape(SLOTS, 4, 128)
    faces = occ.reshape(SLOTS, 8, 2, 4, 8)
    up = jnp.roll(faces[:, 7].transpose(0, 2, 1, 3), 3, axis=1)
    down = faces[:, 0].transpose(0, 2, 1, 3)
    a = jnp.concatenate([occ[:, 4:5], occ[:, 1:4]], axis=1)
    b = jnp.stack(
        [occ[:, 6, 32:], occ[:, 5, :32], occ[:, 6, :32], occ[:, 5, 32:]], axis=1
    )
    packed = [base, up.reshape(SLOTS, 4, 16), down.reshape(SLOTS, 4, 16), a, b]
    packed = jnp.pad(jnp.concatenate(packed, axis=2), ((0, 0), (0, 4), (0, 0)))
    return pl.pallas_call(
        mask_kernel,
        out_shape=(
            jax.ShapeDtypeStruct((SLOTS, 20, 8, 128), F32),
            jax.ShapeDtypeStruct((SLOTS, 12, 8, 128), F32),
        ),
        name="masks",
        compiler_params=pltpu.CompilerParams(vmem_limit_bytes=GRANT),
        cost_estimate=pl.CostEstimate(
            flops=2**20, bytes_accessed=4 * 2**20, transcendentals=0
        ),
    )(packed)


def weight_kernel(w_ref, out_ref):
    h = pl.program_id(0)
    row = lax.broadcasted_iota(jnp.int32, (32, 128), 0) + 32 * h
    lanes = lane_ids((32, 128))
    low = lanes < 64
    eye = (lanes % 64 == row).astype(F32)
    zero = jnp.zeros((32, 128), F32)
    channels = pl.ds(pl.multiple_of(32 * h, 32), 32)
    for jk in range(9):
        taps = [w_ref[9 * i + jk, channels, :] for i in range(3)]
        if jk == 4:
            taps[1] = taps[1] + eye
        taps = taps + [zero]
        window = [split(jnp.where(low, taps[d], taps[d - 1])) for d in range(4)]
        for kind, order in enumerate(((1, 2, 3, 0), (3, 0, 1, 2))):
            hi = jnp.concatenate([window[d][0] for d in order], axis=0)
            lo = jnp.concatenate([window[d][1] for d in order], axis=0)
            at = 256 * jk
            out_ref[0, kind, at : at + 128, :128] = hi
            out_ref[0, kind, at : at + 128, 128:] = lo
            out_ref[0, kind, at + 128 : at + 256, :128] = lo
            out_ref[0, kind, at + 128 : at + 256, 128:] = hi


def weight_tables(weights):
    w = weights.reshape(27, 64, 64)
    return pl.pallas_call(
        weight_kernel,
        out_shape=jax.ShapeDtypeStruct((2, 2, 18 * 128, 256), BF16),
        grid=(2,),
        in_specs=[pl.BlockSpec(memory_space=pltpu.VMEM)],
        out_specs=pl.BlockSpec((1, 2, 18 * 128, 256), lambda h: (h, 0, 0, 0)),
        name="weights",
        compiler_params=pltpu.CompilerParams(vmem_limit_bytes=GRANT),
        cost_estimate=pl.CostEstimate(
            flops=2**20, bytes_accessed=6 * 2**20, transcendentals=0
        ),
    )(jnp.concatenate([w, w], axis=2))


def owner(receive, occupancy, neighbours, own_rank, weight_one, bias_one, shift):
    mask_first, mask_second = mask_tables(occupancy)
    tables = weight_tables(weight_one)
    bias = jnp.broadcast_to(bias_one[:, None], (64, 128))
    present = neighbours >= 0
    local = neighbours % SLOTS
    away = (neighbours // SLOTS != own_rank).astype(jnp.int32) * SLOTS
    ids = jnp.where(present, local, -1)
    slots = jnp.arange(SLOTS, dtype=jnp.int32)
    perms = (ids[:, 2:].T[:, :, None] == slots).astype(BF16)
    wide = jnp.where(present, local + away, -SLOTS * 8)[:, :2].T[:, None, :] * 8
    wide = wide + jnp.arange(8, dtype=jnp.int32)[:, None]
    places = jnp.arange(2 * ROWS, dtype=jnp.int32)
    perms_x = (wide.reshape(2, ROWS)[:, :, None] == places).astype(BF16)
    rows = receive(0, ()).reshape(SLOTS, 20, 8, 128)
    ready = (mask_first, mask_second, tables, perms, perms_x, bias)
    later = receive(1, ready).reshape(SLOTS, 12, 8, 128)
    rows, up, down = planes(rows, mask_first)
    ends = (perms_x, up, down, shift(up, 1), shift(down, -1))
    kept_mid = early(True, rows, perms, tables)
    kept_ends = early(False, rows, perms, tables, ends)
    return late(
        later, mask_second, perms, tables, ends, kept_mid, kept_ends, occupancy, bias
    )


def shards(features, send_pick, occupancy, neighbours, weight_one, bias_one):
    def receive(h, after):
        outgoing = pack(h, send_pick, features, after)
        return lax.all_to_all(outgoing, "gx", split_axis=0, concat_axis=0, tiled=True)

    own_rank = lax.axis_index(("gx", "gy"))
    return owner(
        receive,
        occupancy,
        neighbours,
        own_rank,
        weight_one,
        bias_one,
        lambda block, distance: passed_along(block, ("gx", "gy"), distance),
    )


def solution(mesh):
    in_specs = (
        P(("gx", "gy"), None, None),
        P(("gx", "gy"), None),
        P(("gx", "gy"), None),
        P(("gx", "gy"), None),
        P(),
        P(),
    )
    out_specs = P(("gx", "gy"), None, None)
    return jax.shard_map(shards, mesh=mesh, in_specs=in_specs, out_specs=out_specs, check_vma=False)
```

```python
import jax
import jax.numpy as jnp
from jax import lax
from jax.experimental import pallas as pl
from jax.experimental.pallas import tpu as pltpu
from jax.sharding import PartitionSpec as P

F32 = jnp.float32
BF16 = jnp.bfloat16
SLOTS = 32
SRC = 16
ROWS = 8 * SLOTS
GRANT = 67043328


def passed_along(block, axis, distance):
    devices = range(lax.axis_size(axis))
    route = [(i - distance, i) for i in devices if i - distance in devices]
    return lax.ppermute(block, axis, route)


def lane_ids(shape):
    return lax.broadcasted_iota(jnp.int32, shape, len(shape) - 1)


def split(v):
    hi = v.astype(BF16)
    return hi, (v - hi.astype(F32)).astype(BF16)


def turned(x_ref, r, channels):
    low = lane_ids((32, 128)) < 64
    groups = []
    for g in range(4):
        p = g // 2
        a = x_ref[r, channels, p * 128 : (p + 1) * 128]
        b = x_ref[r, channels, (p + 2) * 128 : (p + 3) * 128]
        if g % 2 == 0:
            groups.append(jnp.where(low, a, pltpu.roll(b, 64, 1)))
        else:
            groups.append(jnp.where(low, pltpu.roll(a, 64, 1), b))
    return jnp.concatenate(groups, axis=0).T


def pack_first(x_ref, t_ref):
    channels = slice(32, 64)
    low = lane_ids((32, 128)) < 64
    group = lane_ids((8, 128)) // 32
    both = []
    for r in range(4):
        t_ref[r, :128] = turned(x_ref, r, slice(0, 32))
        both.append(jnp.where(low, x_ref[r, channels, :128], x_ref[r, channels, 384:]))
    planes_t = jnp.concatenate(both, axis=0).T
    for r in range(4):
        for plane in range(2):
            for q in range(2):
                value = None
                for g in range(4):
                    at = (1 - plane) * 64 + (4 * q + g) * 8
                    to = (g + 3) % 4 if plane == 0 else g
                    tile = planes_t[at : at + 8]
                    if to != r:
                        tile = pltpu.roll(tile, (32 * (to - r)) % 128, 1)
                    value = tile if value is None else jnp.where(group == to, tile, value)
                at = 128 + (2 * plane + q) * 8
                t_ref[r, at : at + 8] = value


def pack_second(x_ref, t_ref):
    group = lane_ids((64, 128)) // 32
    group_b = lane_ids((32, 128)) // 32
    inner = (group_b == 1) | (group_b == 2)
    for r in range(4):
        t = turned(x_ref, r, slice(32, 64))
        t_ref[r, :64] = jnp.where(group == 0, t[64:], t[:64])
        t_ref[r, 64:96] = jnp.where(inner, t[64:96], pltpu.roll(t[96:], 64, 1))


def pack_kernel(half, pick_ref, x_ref, *refs):
    out_ref, t_ref, slot_ref, sem = refs[-4:]
    n = pl.program_id(0)

    @pl.when(n == 0)
    def _():
        for j in range(SLOTS):
            p = pick_ref[0, j]
            slot_ref[jnp.where(p < 0, SRC, p)] = j

    (pack_second if half else pack_first)(x_ref, t_ref.at[pl.ds(4 * n, 4)])

    def copy(r):
        return pltpu.make_async_copy(t_ref.at[r], out_ref.at[slot_ref[r]], sem.at[r])

    for r in range(4):
        copy(4 * n + r).start()

    @pl.when(n == 3)
    def _():
        for r in range(SRC):
            copy(r).wait()


def pack(half, send_pick, features, after):
    rows = 96 if half else 160
    return pl.pallas_call(
        lambda *refs: pack_kernel(half, *refs),
        out_shape=jax.ShapeDtypeStruct((SLOTS, rows, 128), F32),
        grid=(4,),
        in_specs=[
            pl.BlockSpec(memory_space=pltpu.SMEM),
            pl.BlockSpec((4, 64, 512), lambda n: (n, 0, 0)),
        ]
        + [pl.BlockSpec(memory_space=pl.ANY)] * len(after),
        out_specs=pl.BlockSpec(memory_space=pl.ANY),
        scratch_shapes=[
            pltpu.VMEM((SRC, rows, 128), F32),
            pltpu.SMEM((SLOTS,), jnp.int32),
            pltpu.SemaphoreType.DMA((SRC,)),
        ],
        name=f"pack{half}",
        compiler_params=pltpu.CompilerParams(vmem_limit_bytes=GRANT),
        cost_estimate=pl.CostEstimate(
            flops=0, bytes_accessed=6 * 2**20, transcendentals=0
        ),
    )(send_pick, features, *after)


def masked(r_ref, m_ref, at, tile):
    rows = jnp.where(m_ref[at, tile] > 0, r_ref[at, tile], 0.0)
    return rows.reshape(rows.shape[0] * 8, 128)


def tile_rows(v_ref, tile):
    return v_ref[:, tile].reshape(ROWS, 128)


def planes_kernel(r_ref, m_ref, v_ref, up_ref, down_ref):
    group = lane_ids((32, 128)) // 32

    for c in range(2):
        bricks = slice(c * 4, c * 4 + 4)
        out = slice(c * 32, c * 32 + 32)
        for q in range(2):
            up = jnp.zeros((32, 128), F32)
            down = jnp.zeros((32, 128), F32)
            for g in range(4):
                tile = 4 * q + g
                v0 = masked(r_ref, m_ref, bricks, tile)
                v1 = masked(r_ref, m_ref, bricks, tile + 8)
                v_ref[bricks, tile] = v0.reshape(4, 8, 128)
                v_ref[bricks, tile + 8] = v1.reshape(4, 8, 128)
                v0 = pltpu.roll(v0, 32 * g, 1) if g else v0
                v1 = pltpu.roll(v1, 32 * g, 1) if g else v1
                up = jnp.where(group == (g + 3) % 4, v1, up)
                down = jnp.where(group == g, v0, down)
            up_ref[0, q, out, :] = up
            down_ref[0, q, out, :] = down
            up_ref[1, q, out, :] = masked(r_ref, m_ref, bricks, 16 + q)
            down_ref[1, q, out, :] = masked(r_ref, m_ref, bricks, 18 + q)


def planes(rows, mask_rows):
    shape = jax.ShapeDtypeStruct((2, 2, ROWS, 128), F32)
    tiles = pl.BlockSpec((8, 20, 8, 128), lambda n: (n, 0, 0, 0))
    brick = pl.BlockSpec((8, 16, 8, 128), lambda n: (n, 0, 0, 0))
    plane = pl.BlockSpec((2, 2, 64, 128), lambda n: (0, 0, n, 0))
    return pl.pallas_call(
        planes_kernel,
        out_shape=(jax.ShapeDtypeStruct((SLOTS, 16, 8, 128), F32), shape, shape),
        grid=(4,),
        in_specs=[tiles, tiles],
        out_specs=(brick, plane, plane),
        name="planes",
        compiler_params=pltpu.CompilerParams(vmem_limit_bytes=GRANT),
        cost_estimate=pl.CostEstimate(
            flops=2**20, bytes_accessed=8 * 2**20, transcendentals=0
        ),
    )(rows, mask_rows)


def order_tables(order_ref):
    row = lax.broadcasted_iota(jnp.int32, (ROWS, ROWS), 0)
    column = lane_ids((ROWS, ROWS))
    forth = (((row & 31) << 3) | (row >> 5)) == column
    back = (((row & 7) << 5) | (row >> 3)) == column
    order_ref[0] = forth.astype(F32).astype(BF16)
    order_ref[1] = back.astype(F32).astype(BF16)


def moved_rows(order, value):
    both = jnp.concatenate(split(value), axis=1)
    return jnp.dot(order, both, preferred_element_type=F32)


def sides(p_ref, f_hi, f_lo):
    def spread(which, sources, targets):
        blocks = [f[y, z] for f in (f_hi, f_lo) for y, z in sources]
        moved = jnp.dot(
            p_ref[which], jnp.concatenate(blocks, axis=1), preferred_element_type=F32
        )
        n = 0
        for f in (f_hi, f_lo):
            for y, z in targets:
                f[y, z] = moved[:, n * 128 : (n + 1) * 128].astype(BF16)
                n += 1

    inner = range(1, 9)
    spread(0, [(8, z) for z in inner], [(0, z) for z in inner])
    spread(1, [(1, z) for z in inner], [(9, z) for z in inner])
    spread(2, [(y, 8) for y in range(10)], [(y, 0) for y in range(10)])
    spread(3, [(y, 1) for y in range(10)], [(y, 9) for y in range(10)])


def put(f_hi, f_lo, y, hi, lo):
    f_hi[y + 1, 1:9] = hi.astype(BF16).reshape(8, SLOTS, 128)
    f_lo[y + 1, 1:9] = lo.astype(BF16).reshape(8, SLOTS, 128)


def fill_mid(i, v_ref, order_ref, f_hi, f_lo):
    upper = lane_ids((ROWS, 128)) < 32 + 64 * i

    def one(y, carry):
        v0 = tile_rows(v_ref, y)
        v1 = tile_rows(v_ref, 8 + y)
        moved = moved_rows(order_ref[0], jnp.where(upper, v1, v0))
        put(f_hi, f_lo, y, moved[:, :128], moved[:, 128:])
        return carry

    lax.fori_loop(0, 8, one, 0, unroll=8)


def fill_ends(i, v_ref, px_ref, up, down, low, high, order_ref, halo, f_hi, f_lo):
    outer = lane_ids((ROWS, 128)) // 32 == 3 - 3 * i
    for q in range(2):
        near = jnp.where(i == 0, up[0, q], down[0, q])
        far = jnp.where(i == 0, low[0, q], high[0, q])
        halo[q] = moved_rows(px_ref[0], jnp.concatenate([near, far], axis=0))

    def one(q, carry):
        for g in range(4):
            y = q * 4 + g
            moved = moved_rows(order_ref[0], tile_rows(v_ref, 8 * i + y))
            parts = []
            for part in range(2):
                side = halo[q, :, 128 * part : 128 * part + 128]
                side = pltpu.roll(side, 128 - 32 * g, 1) if g else side
                parts.append(
                    jnp.where(outer, side, moved[:, 128 * part : 128 * part + 128])
                )
            put(f_hi, f_lo, y, *parts)
        return carry

    lax.fori_loop(0, 2, one, 0, unroll=2)


def inner_rows(m, y, r_ref, m_ref):
    group = lane_ids((ROWS, 128)) // 32
    every = slice(None)
    a = masked(r_ref, m_ref, every, y)
    b = masked(r_ref, m_ref, every, 8 + y % 4)
    b = pltpu.roll(b, 64, 1) if y > 3 else b
    return jnp.where((m >= 2) & ((group == 1) | (group == 2)), b, a)


def fill_inner(m, r_ref, m_ref, order_ref, f_hi, f_lo):
    for y in range(8):
        moved = moved_rows(order_ref[0], inner_rows(m, y, r_ref, m_ref))
        put(f_hi, f_lo, y, moved[:, :128], moved[:, 128:])


def fill_outer(m, r_ref, m_ref, px_ref, up, down, low, high, order_ref, halo, f_hi, f_lo):
    group = lane_ids((ROWS, 128)) // 32
    outer = group == jnp.where(m == 0, 3, 0)
    edge = group == jnp.where(m == 0, 0, 3)
    for q in range(2):
        own = jnp.where(m == 0, down[0, q], up[0, q])
        near = jnp.where(m == 0, up[0, q], down[0, q])
        far = jnp.where(m == 0, low[0, q], high[0, q])
        halo[q] = moved_rows(px_ref[0], jnp.concatenate([near, far], axis=0))
        halo[2 + q] = moved_rows(order_ref[0], own)
    for y in range(8):
        q, g = y // 4, y % 4
        moved = moved_rows(order_ref[0], inner_rows(m, y, r_ref, m_ref))
        parts = []
        for part in range(2):
            lanes = slice(128 * part, 128 * part + 128)
            side, own = halo[q, :, lanes], halo[2 + q, :, lanes]
            if g:
                side = pltpu.roll(side, 128 - 32 * g, 1)
                own = pltpu.roll(own, 128 - 32 * g, 1)
            value = jnp.where(outer, side, moved[:, lanes])
            parts.append(jnp.where(edge, own, value))
        put(f_hi, f_lo, y, *parts)


def convolve(f_hi, f_lo, w_ref, store, beside=lambda t: None):
    for t in range(4):
        parts = []
        for j in range(3):
            for k in range(3):
                for f in (f_hi, f_lo):
                    rows = f[2 * t + j : 2 * t + j + 2, k : k + 8]
                    parts.append(rows.reshape(2 * ROWS, 128))
        both = jnp.dot(
            jnp.concatenate(parts, axis=1), w_ref[0, 0], preferred_element_type=F32
        )
        beside(t)
        for d in range(2):
            at = slice(d * ROWS, (d + 1) * ROWS)
            store(2 * t + d, both[at, :128] + both[at, 128:])


def by_brick(order_ref, sum_ref, acc_ref):
    for y in range(8):
        back = moved_rows(order_ref[1], sum_ref[y * ROWS : (y + 1) * ROWS, :])
        acc_ref[:, y] = (back[:, :128] + back[:, 128:]).reshape(SLOTS, 8, 128)


def finish_pair(n, acc_ref, occ_ref, bias, out_ref):
    low = lane_ids((64, 128)) < 64
    b = 2 * n
    t = acc_ref[b : b + 2].reshape(128, 128).T
    even, odd = t[:64], t[64:]
    first = jnp.where(low, even, pltpu.roll(odd, 64, 1))
    second = jnp.where(low, pltpu.roll(even, 64, 1), odd)
    for d, value in enumerate((first, second)):
        mask = occ_ref[b + d : b + d + 1, :].astype(F32)
        out_ref[b + d] = mask * jnp.maximum(value + bias, 0.0)


def early_body(mid, refs):
    i = pl.program_id(0)
    v_ref, p_ref, w_ref, *refs = refs
    extra = []
    if not mid:
        extra, refs = refs[:5], refs[5:]
    out_ref, f_hi, f_lo, order_ref, halo = refs

    @pl.when(i == 0)
    def _():
        order_tables(order_ref)

    if mid:
        fill_mid(i, v_ref, order_ref, f_hi, f_lo)
    else:
        fill_ends(i, v_ref, *extra, order_ref, halo, f_hi, f_lo)
    sides(p_ref, f_hi, f_lo)

    def store(y, value):
        out_ref[0, y * ROWS : (y + 1) * ROWS, :] = value

    convolve(f_hi, f_lo, w_ref, store)


def late_body(*refs):
    r_ref, m_ref, p_ref, w_ref, *refs = refs
    sides_refs, refs = refs[:5], refs[5:]
    acc_mid, acc_ends, occ_ref, bias_ref, out_ref, *refs = refs
    f_hi, f_lo, order_ref, halo, sum_ref, acc_ref = refs
    m = pl.program_id(0)
    mid = (m == 1) | (m == 2)

    @pl.when(m == 0)
    def _():
        order_tables(order_ref)

    @pl.when(mid)
    def _():
        fill_inner(m, r_ref, m_ref, order_ref, f_hi, f_lo)

    @pl.when((m == 0) | (m == 3))
    def _():
        fill_outer(m, r_ref, m_ref, *sides_refs, order_ref, halo, f_hi, f_lo)

    def store(y, value):
        at = slice(y * ROWS, (y + 1) * ROWS)
        sum_ref[at, :] = value + jnp.where(mid, acc_mid[0, at, :], acc_ends[0, at, :])

    def before(t):
        bias = bias_ref[...]
        for n in range(4 * t, 4 * t + 4):
            finish_pair(n, acc_ref, occ_ref, bias, out_ref)

    @pl.when(m < 4)
    def _():
        sides(p_ref, f_hi, f_lo)
        convolve(f_hi, f_lo, w_ref, store, before)
        by_brick(order_ref, sum_ref, acc_ref)

    @pl.when(m == 4)
    def _():
        for t in range(4):
            before(t)


VMEM = pl.BlockSpec(memory_space=pltpu.VMEM)
FIELDS = [pltpu.VMEM((10, 10, SLOTS, 128), BF16)] * 2 + [pltpu.VMEM((2, ROWS, ROWS), BF16)]
PARAMS = pltpu.CompilerParams(vmem_limit_bytes=GRANT)


def half_of(h):
    return pl.BlockSpec((1, 2, ROWS, 128), lambda i: (h, 0, 0, 0))


def early(mid, rows, perms, weights, ends=()):
    kind = (lambda i: 1 - i) if mid else (lambda i: i)
    operands = [rows, perms, weights]
    specs = [VMEM, VMEM, pl.BlockSpec((1, 1, 18 * 128, 256), lambda i: (0, kind(i), 0, 0))]
    if not mid:
        operands += list(ends)
        specs += [pl.BlockSpec((1, ROWS, 2 * ROWS), lambda i: (i, 0, 0))] + [half_of(0)] * 4
    return pl.pallas_call(
        lambda *refs: early_body(mid, refs),
        out_shape=jax.ShapeDtypeStruct((2, 64 * SLOTS, 128), F32),
        grid=(2,),
        in_specs=specs,
        out_specs=pl.BlockSpec((1, 64 * SLOTS, 128), lambda i: (i, 0, 0)),
        scratch_shapes=FIELDS + [pltpu.VMEM((2, ROWS, ROWS), F32)],
        compiler_params=PARAMS,
        name="mid" if mid else "ends",
        cost_estimate=pl.CostEstimate(
            flops=2 * 2 * 2048 * 2304 * 256, bytes_accessed=8 * 2**20, transcendentals=0
        ),
    )(*operands)


def late(rows, mask_rows, perms, weights, ends, kept_mid, kept_ends, occupancy, bias):
    acc = (1, 64 * SLOTS, 128)
    specs = [VMEM, VMEM, VMEM]
    specs += [pl.BlockSpec((1, 1, 18 * 128, 256), lambda m: (1, m % 2, 0, 0))]
    specs += [pl.BlockSpec((1, ROWS, 2 * ROWS), lambda m: (jnp.minimum(m // 2, 1), 0, 0))]
    specs += [half_of(1)] * 4
    specs += [pl.BlockSpec(acc, lambda m: (jnp.minimum(m // 2, 1), 0, 0))]
    specs += [pl.BlockSpec(acc, lambda m: (m // 3, 0, 0))]
    specs += [pl.BlockSpec((SLOTS, 128), lambda m: (0, jnp.maximum(m - 1, 0))), VMEM]
    return pl.pallas_call(
        lambda *refs: late_body(*refs),
        out_shape=jax.ShapeDtypeStruct((SLOTS, 64, 512), F32),
        grid=(5,),
        in_specs=specs,
        out_specs=pl.BlockSpec((SLOTS, 64, 128), lambda m: (0, 0, jnp.maximum(m - 1, 0))),
        scratch_shapes=FIELDS
        + [
            pltpu.VMEM((4, ROWS, ROWS), F32),
            pltpu.VMEM(acc[1:], F32),
            pltpu.VMEM((SLOTS, 8, 8, 128), F32),
        ],
        compiler_params=PARAMS,
        name="late",
        cost_estimate=pl.CostEstimate(
            flops=4 * 2 * 2048 * 2304 * 256, bytes_accessed=16 * 2**20, transcendentals=0
        ),
    )(rows, mask_rows, perms, weights, *ends, kept_mid, kept_ends, occupancy, bias)


def mask_kernel(occ_ref, first_ref, second_ref):
    group = lax.broadcasted_iota(jnp.int32, (8, 128), 0)
    spread = (lane_ids((8, 128)) // 32 == group).astype(F32)

    def one(b, carry):
        rows = jnp.dot(occ_ref[b].T, spread, preferred_element_type=F32)
        first_ref[b] = rows[:160].reshape(20, 8, 128)
        second_ref[b] = rows[160:].reshape(12, 8, 128)
        return carry

    lax.fori_loop(0, SLOTS, one, 0, unroll=2)


def mask_tables(occupancy):
    occ = occupancy.astype(F32).reshape(SLOTS, 8, 64)
    base = occ.reshape(SLOTS, 2, 4, 64).transpose(0, 2, 1, 3).reshape(SLOTS, 4, 128)
    faces = occ.reshape(SLOTS, 8, 2, 4, 8)
    up = jnp.roll(faces[:, 7].transpose(0, 2, 1, 3), 3, axis=1)
    down = faces[:, 0].transpose(0, 2, 1, 3)
    a = jnp.concatenate([occ[:, 4:5], occ[:, 1:4]], axis=1)
    b = jnp.stack(
        [occ[:, 6, 32:], occ[:, 5, :32], occ[:, 6, :32], occ[:, 5, 32:]], axis=1
    )
    packed = [base, up.reshape(SLOTS, 4, 16), down.reshape(SLOTS, 4, 16), a, b]
    packed = jnp.pad(jnp.concatenate(packed, axis=2), ((0, 0), (0, 4), (0, 0)))
    return pl.pallas_call(
        mask_kernel,
        out_shape=(
            jax.ShapeDtypeStruct((SLOTS, 20, 8, 128), F32),
            jax.ShapeDtypeStruct((SLOTS, 12, 8, 128), F32),
        ),
        name="masks",
        compiler_params=pltpu.CompilerParams(vmem_limit_bytes=GRANT),
        cost_estimate=pl.CostEstimate(
            flops=2**20, bytes_accessed=4 * 2**20, transcendentals=0
        ),
    )(packed)


def weight_kernel(w_ref, out_ref):
    h = pl.program_id(0)
    row = lax.broadcasted_iota(jnp.int32, (32, 128), 0) + 32 * h
    lanes = lane_ids((32, 128))
    low = lanes < 64
    eye = (lanes % 64 == row).astype(F32)
    zero = jnp.zeros((32, 128), F32)
    channels = pl.ds(pl.multiple_of(32 * h, 32), 32)
    for jk in range(9):
        taps = [w_ref[9 * i + jk, channels, :] for i in range(3)]
        if jk == 4:
            taps[1] = taps[1] + eye
        taps = taps + [zero]
        window = [split(jnp.where(low, taps[d], taps[d - 1])) for d in range(4)]
        for kind, order in enumerate(((1, 2, 3, 0), (3, 0, 1, 2))):
            hi = jnp.concatenate([window[d][0] for d in order], axis=0)
            lo = jnp.concatenate([window[d][1] for d in order], axis=0)
            at = 256 * jk
            out_ref[0, kind, at : at + 128, :128] = hi
            out_ref[0, kind, at : at + 128, 128:] = lo
            out_ref[0, kind, at + 128 : at + 256, :128] = lo
            out_ref[0, kind, at + 128 : at + 256, 128:] = hi


def weight_tables(weights):
    w = weights.reshape(27, 64, 64)
    return pl.pallas_call(
        weight_kernel,
        out_shape=jax.ShapeDtypeStruct((2, 2, 18 * 128, 256), BF16),
        grid=(2,),
        in_specs=[pl.BlockSpec(memory_space=pltpu.VMEM)],
        out_specs=pl.BlockSpec((1, 2, 18 * 128, 256), lambda h: (h, 0, 0, 0)),
        name="weights",
        compiler_params=pltpu.CompilerParams(vmem_limit_bytes=GRANT),
        cost_estimate=pl.CostEstimate(
            flops=2**20, bytes_accessed=6 * 2**20, transcendentals=0
        ),
    )(jnp.concatenate([w, w], axis=2))


def owner(receive, occupancy, neighbours, own_rank, weight_one, bias_one, shift):
    mask_first, mask_second = mask_tables(occupancy)
    tables = weight_tables(weight_one)
    bias = jnp.broadcast_to(bias_one[:, None], (64, 128))
    present = neighbours >= 0
    local = neighbours % SLOTS
    away = (neighbours // SLOTS != own_rank).astype(jnp.int32) * SLOTS
    ids = jnp.where(present, local, -1)
    slots = jnp.arange(SLOTS, dtype=jnp.int32)
    perms = (ids[:, 2:].T[:, :, None] == slots).astype(BF16)
    wide = jnp.where(present, local + away, -SLOTS * 8)[:, :2].T[:, None, :] * 8
    wide = wide + jnp.arange(8, dtype=jnp.int32)[:, None]
    places = jnp.arange(2 * ROWS, dtype=jnp.int32)
    perms_x = (wide.reshape(2, ROWS)[:, :, None] == places).astype(BF16)
    rows = receive(0, ()).reshape(SLOTS, 20, 8, 128)
    ready = (mask_first, mask_second, tables, perms, perms_x, bias)
    later = receive(1, ready).reshape(SLOTS, 12, 8, 128)
    rows, up, down = planes(rows, mask_first)
    ends = (perms_x, up, down, shift(up, 1), shift(down, -1))
    kept_mid = early(True, rows, perms, tables)
    kept_ends = early(False, rows, perms, tables, ends)
    return late(
        later, mask_second, perms, tables, ends, kept_mid, kept_ends, occupancy, bias
    )


def shards(features, send_pick, occupancy, neighbours, weight_one, bias_one):
    def receive(h, after):
        outgoing = pack(h, send_pick, features, after)
        return lax.all_to_all(outgoing, "gx", split_axis=0, concat_axis=0, tiled=True)

    own_rank = lax.axis_index(("gx", "gy"))
    return owner(
        receive,
        occupancy,
        neighbours,
        own_rank,
        weight_one,
        bias_one,
        lambda block, distance: passed_along(block, ("gx", "gy"), distance),
    )


def solution(mesh):
    in_specs = (
        P(("gx", "gy"), None, None),
        P(("gx", "gy"), None),
        P(("gx", "gy"), None),
        P(("gx", "gy"), None),
        P(),
        P(),
    )
    out_specs = P(("gx", "gy"), None, None)
    return jax.shard_map(shards, mesh=mesh, in_specs=in_specs, out_specs=out_specs, check_vma=False)
```

```python
import jax
import jax.numpy as jnp
from jax import lax
from jax.experimental import pallas as pl
from jax.experimental.pallas import tpu as pltpu
from jax.sharding import PartitionSpec as P

F32 = jnp.float32
BF16 = jnp.bfloat16
SLOTS = 32
SRC = 16
ROWS = 8 * SLOTS
GRANT = 67043328
PACK = 8
PLANE = 16


def passed_along(block, axis, distance):
    devices = range(lax.axis_size(axis))
    route = [(i - distance, i) for i in devices if i - distance in devices]
    return lax.ppermute(block, axis, route)


def lane_ids(shape):
    return lax.broadcasted_iota(jnp.int32, shape, len(shape) - 1)


def split(v):
    hi = v.astype(BF16)
    return hi, (v - hi.astype(F32)).astype(BF16)


def turned(x_ref, r, channels):
    low = lane_ids((32, 128)) < 64
    groups = []
    for g in range(4):
        p = g // 2
        a = x_ref[r, channels, p * 128 : (p + 1) * 128]
        b = x_ref[r, channels, (p + 2) * 128 : (p + 3) * 128]
        if g % 2 == 0:
            groups.append(jnp.where(low, a, pltpu.roll(b, 64, 1)))
        else:
            groups.append(jnp.where(low, pltpu.roll(a, 64, 1), b))
    return jnp.concatenate(groups, axis=0).T


def pack_first(x_ref, t_ref):
    channels = slice(32, 64)
    low = lane_ids((32, 128)) < 64
    group = lane_ids((8, 128)) // 32
    for first in range(0, PACK, 4):
        both = []
        for r in range(first, first + 4):
            t_ref[r, :128] = turned(x_ref, r, slice(0, 32))
            both.append(
                jnp.where(low, x_ref[r, channels, :128], x_ref[r, channels, 384:])
            )
        planes_t = jnp.concatenate(both, axis=0).T
        for r in range(4):
            for plane in range(2):
                for q in range(2):
                    value = None
                    for g in range(4):
                        at = (1 - plane) * 64 + (4 * q + g) * 8
                        to = (g + 3) % 4 if plane == 0 else g
                        tile = planes_t[at : at + 8]
                        if to != r:
                            tile = pltpu.roll(tile, (32 * (to - r)) % 128, 1)
                        if value is not None:
                            tile = jnp.where(group == to, tile, value)
                        value = tile
                    at = 128 + (2 * plane + q) * 8
                    t_ref[first + r, at : at + 8] = value


def pack_second(x_ref, t_ref):
    group = lane_ids((64, 128)) // 32
    group_b = lane_ids((32, 128)) // 32
    inner = (group_b == 1) | (group_b == 2)
    for r in range(PACK):
        t = turned(x_ref, r, slice(32, 64))
        t_ref[r, :64] = jnp.where(group == 0, t[64:], t[:64])
        t_ref[r, 64:96] = jnp.where(inner, t[64:96], pltpu.roll(t[96:], 64, 1))


def pack_kernel(half, pick_ref, x_ref, *refs):
    out_ref, t_ref, slot_ref, sem = refs[-4:]
    n = pl.program_id(0)

    @pl.when(n == 0)
    def _():
        for j in range(SLOTS):
            p = pick_ref[0, j]
            slot_ref[jnp.where(p < 0, SRC, p)] = j

    (pack_second if half else pack_first)(x_ref, t_ref.at[pl.ds(PACK * n, PACK)])

    def copy(r):
        return pltpu.make_async_copy(t_ref.at[r], out_ref.at[slot_ref[r]], sem.at[r])

    for r in range(PACK):
        copy(PACK * n + r).start()

    @pl.when(n == SRC // PACK - 1)
    def _():
        for r in range(SRC):
            copy(r).wait()


def pack(half, send_pick, features, after):
    rows = 96 if half else 160
    return pl.pallas_call(
        lambda *refs: pack_kernel(half, *refs),
        out_shape=jax.ShapeDtypeStruct((SLOTS, rows, 128), F32),
        grid=(SRC // PACK,),
        in_specs=[
            pl.BlockSpec(memory_space=pltpu.SMEM),
            pl.BlockSpec((PACK, 64, 512), lambda n: (n, 0, 0)),
        ]
        + [pl.BlockSpec(memory_space=pl.ANY)] * len(after),
        out_specs=pl.BlockSpec(memory_space=pl.ANY),
        scratch_shapes=[
            pltpu.VMEM((SRC, rows, 128), F32),
            pltpu.SMEM((SLOTS,), jnp.int32),
            pltpu.SemaphoreType.DMA((SRC,)),
        ],
        name=f"pack{half}",
        compiler_params=pltpu.CompilerParams(vmem_limit_bytes=GRANT),
        cost_estimate=pl.CostEstimate(
            flops=0, bytes_accessed=6 * 2**20, transcendentals=0
        ),
    )(send_pick, features, *after)


def masked(r_ref, m_ref, at, tile):
    rows = jnp.where(m_ref[at, tile] > 0, r_ref[at, tile], 0.0)
    return rows.reshape(rows.shape[0] * 8, 128)


def tile_rows(v_ref, tile):
    return v_ref[:, tile].reshape(ROWS, 128)


def planes_kernel(r_ref, m_ref, v_ref, up_ref, down_ref):
    group = lane_ids((32, 128)) // 32

    for c in range(PLANE // 4):
        bricks = slice(c * 4, c * 4 + 4)
        out = slice(c * 32, c * 32 + 32)
        for q in range(2):
            up = jnp.zeros((32, 128), F32)
            down = jnp.zeros((32, 128), F32)
            for g in range(4):
                tile = 4 * q + g
                v0 = masked(r_ref, m_ref, bricks, tile)
                v1 = masked(r_ref, m_ref, bricks, tile + 8)
                v_ref[bricks, tile] = v0.reshape(4, 8, 128)
                v_ref[bricks, tile + 8] = v1.reshape(4, 8, 128)
                v0 = pltpu.roll(v0, 32 * g, 1) if g else v0
                v1 = pltpu.roll(v1, 32 * g, 1) if g else v1
                up = jnp.where(group == (g + 3) % 4, v1, up)
                down = jnp.where(group == g, v0, down)
            up_ref[0, q, out, :] = up
            down_ref[0, q, out, :] = down
            up_ref[1, q, out, :] = masked(r_ref, m_ref, bricks, 16 + q)
            down_ref[1, q, out, :] = masked(r_ref, m_ref, bricks, 18 + q)


def planes(rows, mask_rows):
    shape = jax.ShapeDtypeStruct((2, 2, ROWS, 128), F32)
    tiles = pl.BlockSpec((PLANE, 20, 8, 128), lambda n: (n, 0, 0, 0))
    brick = pl.BlockSpec((PLANE, 16, 8, 128), lambda n: (n, 0, 0, 0))
    plane = pl.BlockSpec((2, 2, 8 * PLANE, 128), lambda n: (0, 0, n, 0))
    return pl.pallas_call(
        planes_kernel,
        out_shape=(jax.ShapeDtypeStruct((SLOTS, 16, 8, 128), F32), shape, shape),
        grid=(SLOTS // PLANE,),
        in_specs=[tiles, tiles],
        out_specs=(brick, plane, plane),
        name="planes",
        compiler_params=pltpu.CompilerParams(vmem_limit_bytes=GRANT),
        cost_estimate=pl.CostEstimate(
            flops=2**20, bytes_accessed=8 * 2**20, transcendentals=0
        ),
    )(rows, mask_rows)


def order_tables(order_ref):
    row = lax.broadcasted_iota(jnp.int32, (ROWS, ROWS), 0)
    column = lane_ids((ROWS, ROWS))
    forth = (((row & 31) << 3) | (row >> 5)) == column
    back = (((row & 7) << 5) | (row >> 3)) == column
    order_ref[0] = forth.astype(F32).astype(BF16)
    order_ref[1] = back.astype(F32).astype(BF16)


def moved_rows(order, value):
    both = jnp.concatenate(split(value), axis=1)
    return jnp.dot(order, both, preferred_element_type=F32)


def sides(p_ref, f_hi, f_lo):
    def spread(which, sources, targets):
        blocks = [f[y, z] for f in (f_hi, f_lo) for y, z in sources]
        moved = jnp.dot(
            p_ref[which], jnp.concatenate(blocks, axis=1), preferred_element_type=F32
        )
        n = 0
        for f in (f_hi, f_lo):
            for y, z in targets:
                f[y, z] = moved[:, n * 128 : (n + 1) * 128].astype(BF16)
                n += 1

    inner = range(1, 9)
    spread(0, [(8, z) for z in inner], [(0, z) for z in inner])
    spread(1, [(1, z) for z in inner], [(9, z) for z in inner])
    spread(2, [(y, 8) for y in range(10)], [(y, 0) for y in range(10)])
    spread(3, [(y, 1) for y in range(10)], [(y, 9) for y in range(10)])


def put(f_hi, f_lo, y, hi, lo):
    f_hi[y + 1, 1:9] = hi.astype(BF16).reshape(8, SLOTS, 128)
    f_lo[y + 1, 1:9] = lo.astype(BF16).reshape(8, SLOTS, 128)


def fill_mid(i, v_ref, order_ref, f_hi, f_lo):
    upper = lane_ids((ROWS, 128)) < 32 + 64 * i

    def one(y, carry):
        v0 = tile_rows(v_ref, y)
        v1 = tile_rows(v_ref, 8 + y)
        moved = moved_rows(order_ref[0], jnp.where(upper, v1, v0))
        put(f_hi, f_lo, y, moved[:, :128], moved[:, 128:])
        return carry

    lax.fori_loop(0, 8, one, 0, unroll=8)


def fill_ends(i, v_ref, px_ref, up, down, low, high, order_ref, halo, f_hi, f_lo):
    outer = lane_ids((ROWS, 128)) // 32 == 3 - 3 * i
    for q in range(2):
        near = jnp.where(i == 0, up[0, q], down[0, q])
        far = jnp.where(i == 0, low[0, q], high[0, q])
        halo[q] = moved_rows(px_ref[0], jnp.concatenate([near, far], axis=0))

    def one(q, carry):
        for g in range(4):
            y = q * 4 + g
            moved = moved_rows(order_ref[0], tile_rows(v_ref, 8 * i + y))
            parts = []
            for part in range(2):
                side = halo[q, :, 128 * part : 128 * part + 128]
                side = pltpu.roll(side, 128 - 32 * g, 1) if g else side
                parts.append(
                    jnp.where(outer, side, moved[:, 128 * part : 128 * part + 128])
                )
            put(f_hi, f_lo, y, *parts)
        return carry

    lax.fori_loop(0, 2, one, 0, unroll=2)


def inner_rows(m, y, r_ref, m_ref):
    group = lane_ids((ROWS, 128)) // 32
    every = slice(None)
    a = masked(r_ref, m_ref, every, y)
    b = masked(r_ref, m_ref, every, 8 + y % 4)
    b = pltpu.roll(b, 64, 1) if y > 3 else b
    return jnp.where((m >= 2) & ((group == 1) | (group == 2)), b, a)


def fill_inner(m, r_ref, m_ref, order_ref, f_hi, f_lo):
    for y in range(8):
        moved = moved_rows(order_ref[0], inner_rows(m, y, r_ref, m_ref))
        put(f_hi, f_lo, y, moved[:, :128], moved[:, 128:])


def fill_outer(m, r_ref, m_ref, px_ref, up, down, low, high, order_ref, halo, f_hi, f_lo):
    group = lane_ids((ROWS, 128)) // 32
    outer = group == jnp.where(m == 0, 3, 0)
    edge = group == jnp.where(m == 0, 0, 3)
    for q in range(2):
        own = jnp.where(m == 0, down[0, q], up[0, q])
        near = jnp.where(m == 0, up[0, q], down[0, q])
        far = jnp.where(m == 0, low[0, q], high[0, q])
        halo[q] = moved_rows(px_ref[0], jnp.concatenate([near, far], axis=0))
        halo[2 + q] = moved_rows(order_ref[0], own)
    for y in range(8):
        q, g = y // 4, y % 4
        moved = moved_rows(order_ref[0], inner_rows(m, y, r_ref, m_ref))
        parts = []
        for part in range(2):
            lanes = slice(128 * part, 128 * part + 128)
            side, own = halo[q, :, lanes], halo[2 + q, :, lanes]
            if g:
                side = pltpu.roll(side, 128 - 32 * g, 1)
                own = pltpu.roll(own, 128 - 32 * g, 1)
            value = jnp.where(outer, side, moved[:, lanes])
            parts.append(jnp.where(edge, own, value))
        put(f_hi, f_lo, y, *parts)


def convolve(f_hi, f_lo, w_ref, store, beside=lambda t: None):
    for t in range(4):
        parts = []
        for j in range(3):
            for k in range(3):
                for f in (f_hi, f_lo):
                    rows = f[2 * t + j : 2 * t + j + 2, k : k + 8]
                    parts.append(rows.reshape(2 * ROWS, 128))
        both = jnp.dot(
            jnp.concatenate(parts, axis=1), w_ref[0, 0], preferred_element_type=F32
        )
        beside(t)
        for d in range(2):
            at = slice(d * ROWS, (d + 1) * ROWS)
            store(2 * t + d, both[at, :128] + both[at, 128:])


def by_brick(order_ref, sum_ref, acc_ref):
    for y in range(8):
        back = moved_rows(order_ref[1], sum_ref[y * ROWS : (y + 1) * ROWS, :])
        acc_ref[:, y] = (back[:, :128] + back[:, 128:]).reshape(SLOTS, 8, 128)


def finish_pair(n, acc_ref, occ_ref, bias, out_ref):
    low = lane_ids((64, 128)) < 64
    b = 2 * n
    t = acc_ref[b : b + 2].reshape(128, 128).T
    even, odd = t[:64], t[64:]
    first = jnp.where(low, even, pltpu.roll(odd, 64, 1))
    second = jnp.where(low, pltpu.roll(even, 64, 1), odd)
    for d, value in enumerate((first, second)):
        mask = occ_ref[b + d : b + d + 1, :].astype(F32)
        out_ref[b + d] = mask * jnp.maximum(value + bias, 0.0)


def early_body(mid, refs):
    i = pl.program_id(0)
    v_ref, p_ref, w_ref, *refs = refs
    extra = []
    if not mid:
        extra, refs = refs[:5], refs[5:]
    out_ref, f_hi, f_lo, order_ref, halo = refs

    @pl.when(i == 0)
    def _():
        order_tables(order_ref)

    if mid:
        fill_mid(i, v_ref, order_ref, f_hi, f_lo)
    else:
        fill_ends(i, v_ref, *extra, order_ref, halo, f_hi, f_lo)
    sides(p_ref, f_hi, f_lo)

    def store(y, value):
        out_ref[0, y * ROWS : (y + 1) * ROWS, :] = value

    convolve(f_hi, f_lo, w_ref, store)


def late_body(*refs):
    r_ref, m_ref, p_ref, w_ref, *refs = refs
    sides_refs, refs = refs[:5], refs[5:]
    acc_mid, acc_ends, occ_ref, bias_ref, out_ref, *refs = refs
    f_hi, f_lo, order_ref, halo, sum_ref, acc_ref = refs
    m = pl.program_id(0)
    mid = (m == 1) | (m == 2)

    @pl.when(m == 0)
    def _():
        order_tables(order_ref)

    @pl.when(mid)
    def _():
        fill_inner(m, r_ref, m_ref, order_ref, f_hi, f_lo)

    @pl.when((m == 0) | (m == 3))
    def _():
        fill_outer(m, r_ref, m_ref, *sides_refs, order_ref, halo, f_hi, f_lo)

    def store(y, value):
        at = slice(y * ROWS, (y + 1) * ROWS)
        sum_ref[at, :] = value + jnp.where(mid, acc_mid[0, at, :], acc_ends[0, at, :])

    def before(t):
        bias = bias_ref[...]
        for n in range(4 * t, 4 * t + 4):
            finish_pair(n, acc_ref, occ_ref, bias, out_ref)

    @pl.when(m < 4)
    def _():
        sides(p_ref, f_hi, f_lo)
        convolve(f_hi, f_lo, w_ref, store, before)
        by_brick(order_ref, sum_ref, acc_ref)

    @pl.when(m == 4)
    def _():
        for t in range(4):
            before(t)


VMEM = pl.BlockSpec(memory_space=pltpu.VMEM)
FIELDS = [pltpu.VMEM((10, 10, SLOTS, 128), BF16)] * 2 + [pltpu.VMEM((2, ROWS, ROWS), BF16)]
PARAMS = pltpu.CompilerParams(vmem_limit_bytes=GRANT)


def half_of(h):
    return pl.BlockSpec((1, 2, ROWS, 128), lambda i: (h, 0, 0, 0))


def early(mid, rows, perms, weights, ends=()):
    kind = (lambda i: 1 - i) if mid else (lambda i: i)
    operands = [rows, perms, weights]
    specs = [VMEM, VMEM, pl.BlockSpec((1, 1, 18 * 128, 256), lambda i: (0, kind(i), 0, 0))]
    if not mid:
        operands += list(ends)
        specs += [pl.BlockSpec((1, ROWS, 2 * ROWS), lambda i: (i, 0, 0))] + [half_of(0)] * 4
    return pl.pallas_call(
        lambda *refs: early_body(mid, refs),
        out_shape=jax.ShapeDtypeStruct((2, 64 * SLOTS, 128), F32),
        grid=(2,),
        in_specs=specs,
        out_specs=pl.BlockSpec((1, 64 * SLOTS, 128), lambda i: (i, 0, 0)),
        scratch_shapes=FIELDS + [pltpu.VMEM((2, ROWS, ROWS), F32)],
        compiler_params=PARAMS,
        name="mid" if mid else "ends",
        cost_estimate=pl.CostEstimate(
            flops=2 * 2 * 2048 * 2304 * 256, bytes_accessed=8 * 2**20, transcendentals=0
        ),
    )(*operands)


def late(rows, mask_rows, perms, weights, ends, kept_mid, kept_ends, occupancy, bias):
    acc = (1, 64 * SLOTS, 128)
    specs = [VMEM, VMEM, VMEM]
    specs += [pl.BlockSpec((1, 1, 18 * 128, 256), lambda m: (1, m % 2, 0, 0))]
    specs += [pl.BlockSpec((1, ROWS, 2 * ROWS), lambda m: (jnp.minimum(m // 2, 1), 0, 0))]
    specs += [half_of(1)] * 4
    specs += [pl.BlockSpec(acc, lambda m: (jnp.minimum(m // 2, 1), 0, 0))]
    specs += [pl.BlockSpec(acc, lambda m: (m // 3, 0, 0))]
    specs += [pl.BlockSpec((SLOTS, 128), lambda m: (0, jnp.maximum(m - 1, 0))), VMEM]
    return pl.pallas_call(
        lambda *refs: late_body(*refs),
        out_shape=jax.ShapeDtypeStruct((SLOTS, 64, 512), F32),
        grid=(5,),
        in_specs=specs,
        out_specs=pl.BlockSpec((SLOTS, 64, 128), lambda m: (0, 0, jnp.maximum(m - 1, 0))),
        scratch_shapes=FIELDS
        + [
            pltpu.VMEM((4, ROWS, ROWS), F32),
            pltpu.VMEM(acc[1:], F32),
            pltpu.VMEM((SLOTS, 8, 8, 128), F32),
        ],
        compiler_params=PARAMS,
        name="late",
        cost_estimate=pl.CostEstimate(
            flops=4 * 2 * 2048 * 2304 * 256, bytes_accessed=16 * 2**20, transcendentals=0
        ),
    )(rows, mask_rows, perms, weights, *ends, kept_mid, kept_ends, occupancy, bias)


def mask_kernel(occ_ref, first_ref, second_ref):
    group = lax.broadcasted_iota(jnp.int32, (8, 128), 0)
    spread = (lane_ids((8, 128)) // 32 == group).astype(F32)

    def one(b, carry):
        rows = jnp.dot(occ_ref[b].T, spread, preferred_element_type=F32)
        first_ref[b] = rows[:160].reshape(20, 8, 128)
        second_ref[b] = rows[160:].reshape(12, 8, 128)
        return carry

    lax.fori_loop(0, SLOTS, one, 0, unroll=2)


def mask_tables(occupancy):
    occ = occupancy.astype(F32).reshape(SLOTS, 8, 64)
    base = occ.reshape(SLOTS, 2, 4, 64).transpose(0, 2, 1, 3).reshape(SLOTS, 4, 128)
    faces = occ.reshape(SLOTS, 8, 2, 4, 8)
    up = jnp.roll(faces[:, 7].transpose(0, 2, 1, 3), 3, axis=1)
    down = faces[:, 0].transpose(0, 2, 1, 3)
    a = jnp.concatenate([occ[:, 4:5], occ[:, 1:4]], axis=1)
    b = jnp.stack(
        [occ[:, 6, 32:], occ[:, 5, :32], occ[:, 6, :32], occ[:, 5, 32:]], axis=1
    )
    packed = [base, up.reshape(SLOTS, 4, 16), down.reshape(SLOTS, 4, 16), a, b]
    packed = jnp.pad(jnp.concatenate(packed, axis=2), ((0, 0), (0, 4), (0, 0)))
    return pl.pallas_call(
        mask_kernel,
        out_shape=(
            jax.ShapeDtypeStruct((SLOTS, 20, 8, 128), F32),
            jax.ShapeDtypeStruct((SLOTS, 12, 8, 128), F32),
        ),
        name="masks",
        compiler_params=pltpu.CompilerParams(vmem_limit_bytes=GRANT),
        cost_estimate=pl.CostEstimate(
            flops=2**20, bytes_accessed=4 * 2**20, transcendentals=0
        ),
    )(packed)


def weight_kernel(w_ref, out_ref):
    h = pl.program_id(0)
    row = lax.broadcasted_iota(jnp.int32, (32, 128), 0) + 32 * h
    lanes = lane_ids((32, 128))
    low = lanes < 64
    eye = (lanes % 64 == row).astype(F32)
    zero = jnp.zeros((32, 128), F32)
    channels = pl.ds(pl.multiple_of(32 * h, 32), 32)
    for jk in range(9):
        taps = [w_ref[9 * i + jk, channels, :] for i in range(3)]
        if jk == 4:
            taps[1] = taps[1] + eye
        taps = taps + [zero]
        window = [split(jnp.where(low, taps[d], taps[d - 1])) for d in range(4)]
        for kind, order in enumerate(((1, 2, 3, 0), (3, 0, 1, 2))):
            hi = jnp.concatenate([window[d][0] for d in order], axis=0)
            lo = jnp.concatenate([window[d][1] for d in order], axis=0)
            at = 256 * jk
            out_ref[0, kind, at : at + 128, :128] = hi
            out_ref[0, kind, at : at + 128, 128:] = lo
            out_ref[0, kind, at + 128 : at + 256, :128] = lo
            out_ref[0, kind, at + 128 : at + 256, 128:] = hi


def weight_tables(weights):
    w = weights.reshape(27, 64, 64)
    return pl.pallas_call(
        weight_kernel,
        out_shape=jax.ShapeDtypeStruct((2, 2, 18 * 128, 256), BF16),
        grid=(2,),
        in_specs=[pl.BlockSpec(memory_space=pltpu.VMEM)],
        out_specs=pl.BlockSpec((1, 2, 18 * 128, 256), lambda h: (h, 0, 0, 0)),
        name="weights",
        compiler_params=pltpu.CompilerParams(vmem_limit_bytes=GRANT),
        cost_estimate=pl.CostEstimate(
            flops=2**20, bytes_accessed=6 * 2**20, transcendentals=0
        ),
    )(jnp.concatenate([w, w], axis=2))


def owner(receive, occupancy, neighbours, own_rank, weight_one, bias_one, shift):
    mask_first, mask_second = mask_tables(occupancy)
    tables = weight_tables(weight_one)
    bias = jnp.broadcast_to(bias_one[:, None], (64, 128))
    present = neighbours >= 0
    local = neighbours % SLOTS
    away = (neighbours // SLOTS != own_rank).astype(jnp.int32) * SLOTS
    ids = jnp.where(present, local, -1)
    slots = jnp.arange(SLOTS, dtype=jnp.int32)
    perms = (ids[:, 2:].T[:, :, None] == slots).astype(BF16)
    wide = jnp.where(present, local + away, -SLOTS * 8)[:, :2].T[:, None, :] * 8
    wide = wide + jnp.arange(8, dtype=jnp.int32)[:, None]
    places = jnp.arange(2 * ROWS, dtype=jnp.int32)
    perms_x = (wide.reshape(2, ROWS)[:, :, None] == places).astype(BF16)
    rows = receive(0, ()).reshape(SLOTS, 20, 8, 128)
    ready = (mask_first, mask_second, tables, perms, perms_x, bias)
    later = receive(1, ready).reshape(SLOTS, 12, 8, 128)
    rows, up, down = planes(rows, mask_first)
    ends = (perms_x, up, down, shift(up, 1), shift(down, -1))
    kept_mid = early(True, rows, perms, tables)
    kept_ends = early(False, rows, perms, tables, ends)
    return late(
        later, mask_second, perms, tables, ends, kept_mid, kept_ends, occupancy, bias
    )


def shards(features, send_pick, occupancy, neighbours, weight_one, bias_one):
    def receive(h, after):
        outgoing = pack(h, send_pick, features, after)
        return lax.all_to_all(outgoing, "gx", split_axis=0, concat_axis=0, tiled=True)

    own_rank = lax.axis_index(("gx", "gy"))
    return owner(
        receive,
        occupancy,
        neighbours,
        own_rank,
        weight_one,
        bias_one,
        lambda block, distance: passed_along(block, ("gx", "gy"), distance),
    )


def solution(mesh):
    in_specs = (
        P(("gx", "gy"), None, None),
        P(("gx", "gy"), None),
        P(("gx", "gy"), None),
        P(("gx", "gy"), None),
        P(),
        P(),
    )
    out_specs = P(("gx", "gy"), None, None)
    return jax.shard_map(shards, mesh=mesh, in_specs=in_specs, out_specs=out_specs, check_vma=False)
```

```python
import jax
import jax.numpy as jnp
from jax import lax
from jax.experimental import pallas as pl
from jax.experimental.pallas import tpu as pltpu
from jax.sharding import PartitionSpec as P


F32 = jnp.float32
BF16 = jnp.bfloat16
SLOTS = 32
SRC = 16
ROWS = 8 * SLOTS
GRANT = 67043328
PACK = 8
PLANE = 16


def passed_along(block, axis, distance):
    devices = range(lax.axis_size(axis))
    route = [(i - distance, i) for i in devices if i - distance in devices]
    return lax.ppermute(block, axis, route)


def lane_ids(shape):
    return lax.broadcasted_iota(jnp.int32, shape, len(shape) - 1)


def split(v):
    hi = v.astype(BF16)
    return hi, (v - hi.astype(F32)).astype(BF16)


def turned(x_ref, r, channels):
    low = lane_ids((32, 128)) < 64
    groups = []
    for g in range(4):
        p = g // 2
        a = x_ref[r, channels, p * 128 : (p + 1) * 128]
        b = x_ref[r, channels, (p + 2) * 128 : (p + 3) * 128]
        if g % 2 == 0:
            groups.append(jnp.where(low, a, pltpu.roll(b, 64, 1)))
        else:
            groups.append(jnp.where(low, pltpu.roll(a, 64, 1), b))
    return jnp.concatenate(groups, axis=0).T


def pack_first(x_ref, t_ref):
    channels = slice(32, 64)
    low = lane_ids((32, 128)) < 64
    group = lane_ids((8, 128)) // 32
    for first in range(0, PACK, 4):
        both = []
        for r in range(first, first + 4):
            t_ref[r, :128] = turned(x_ref, r, slice(0, 32))
            both.append(
                jnp.where(low, x_ref[r, channels, :128], x_ref[r, channels, 384:])
            )
        planes_t = jnp.concatenate(both, axis=0).T
        for r in range(4):
            for plane in range(2):
                for q in range(2):
                    value = None
                    for g in range(4):
                        at = (1 - plane) * 64 + (4 * q + g) * 8
                        to = (g + 3) % 4 if plane == 0 else g
                        tile = planes_t[at : at + 8]
                        if to != r:
                            tile = pltpu.roll(tile, (32 * (to - r)) % 128, 1)
                        if value is not None:
                            tile = jnp.where(group == to, tile, value)
                        value = tile
                    at = 128 + (2 * plane + q) * 8
                    t_ref[first + r, at : at + 8] = value


def pack_second(x_ref, t_ref):
    group = lane_ids((64, 128)) // 32
    group_b = lane_ids((32, 128)) // 32
    inner = (group_b == 1) | (group_b == 2)
    for r in range(PACK):
        t = turned(x_ref, r, slice(32, 64))
        t_ref[r, :64] = jnp.where(group == 0, t[64:], t[:64])
        t_ref[r, 64:96] = jnp.where(inner, t[64:96], pltpu.roll(t[96:], 64, 1))


def pack_kernel(half, pick_ref, x_ref, *refs):
    out_ref, t_ref, slot_ref, sem = refs[-4:]
    n = pl.program_id(0)

    @pl.when(n == 0)
    def _():
        for j in range(SLOTS):
            p = pick_ref[0, j]
            slot_ref[jnp.where(p < 0, SRC, p)] = j

    (pack_second if half else pack_first)(x_ref, t_ref.at[pl.ds(PACK * n, PACK)])

    def copy(r):
        return pltpu.make_async_copy(t_ref.at[r], out_ref.at[slot_ref[r]], sem.at[r])

    for r in range(PACK):
        copy(PACK * n + r).start()

    @pl.when(n == SRC // PACK - 1)
    def _():
        for r in range(SRC):
            copy(r).wait()


def pack(half, send_pick, features, after):
    rows = 96 if half else 160
    return pl.pallas_call(
        lambda *refs: pack_kernel(half, *refs),
        out_shape=jax.ShapeDtypeStruct((SLOTS, rows, 128), F32),
        grid=(SRC // PACK,),
        in_specs=[
            pl.BlockSpec(memory_space=pltpu.SMEM),
            pl.BlockSpec((PACK, 64, 512), lambda n: (n, 0, 0)),
        ]
        + [pl.BlockSpec(memory_space=pl.ANY)] * len(after),
        out_specs=pl.BlockSpec(memory_space=pl.ANY),
        scratch_shapes=[
            pltpu.VMEM((SRC, rows, 128), F32),
            pltpu.SMEM((SLOTS,), jnp.int32),
            pltpu.SemaphoreType.DMA((SRC,)),
        ],
        compiler_params=pltpu.CompilerParams(vmem_limit_bytes=GRANT),
        cost_estimate=pl.CostEstimate(
            flops=0, bytes_accessed=6 * 2**20, transcendentals=0
        ),
    )(send_pick, features, *after)


def masked(r_ref, m_ref, at, tile):
    rows = jnp.where(m_ref[at, tile] > 0, r_ref[at, tile], 0.0)
    return rows.reshape(rows.shape[0] * 8, 128)


def tile_rows(v_ref, tile):
    return v_ref[:, tile].reshape(ROWS, 128)


def planes_kernel(r_ref, m_ref, v_ref, up_ref, down_ref):
    group = lane_ids((32, 128)) // 32

    for c in range(PLANE // 4):
        bricks = slice(c * 4, c * 4 + 4)
        out = slice(c * 32, c * 32 + 32)
        for q in range(2):
            up = jnp.zeros((32, 128), F32)
            down = jnp.zeros((32, 128), F32)
            for g in range(4):
                tile = 4 * q + g
                v0 = masked(r_ref, m_ref, bricks, tile)
                v1 = masked(r_ref, m_ref, bricks, tile + 8)
                v_ref[bricks, tile] = v0.reshape(4, 8, 128)
                v_ref[bricks, tile + 8] = v1.reshape(4, 8, 128)
                v0 = pltpu.roll(v0, 32 * g, 1) if g else v0
                v1 = pltpu.roll(v1, 32 * g, 1) if g else v1
                up = jnp.where(group == (g + 3) % 4, v1, up)
                down = jnp.where(group == g, v0, down)
            up_ref[0, q, out, :] = up
            down_ref[0, q, out, :] = down
            up_ref[1, q, out, :] = masked(r_ref, m_ref, bricks, 16 + q)
            down_ref[1, q, out, :] = masked(r_ref, m_ref, bricks, 18 + q)


def planes(rows, mask_rows):
    shape = jax.ShapeDtypeStruct((2, 2, ROWS, 128), F32)
    tiles = pl.BlockSpec((PLANE, 20, 8, 128), lambda n: (n, 0, 0, 0))
    brick = pl.BlockSpec((PLANE, 16, 8, 128), lambda n: (n, 0, 0, 0))
    plane = pl.BlockSpec((2, 2, 8 * PLANE, 128), lambda n: (0, 0, n, 0))
    return pl.pallas_call(
        planes_kernel,
        out_shape=(jax.ShapeDtypeStruct((SLOTS, 16, 8, 128), F32), shape, shape),
        grid=(SLOTS // PLANE,),
        in_specs=[tiles, tiles],
        out_specs=(brick, plane, plane),
        name="planes",
        compiler_params=pltpu.CompilerParams(vmem_limit_bytes=GRANT),
        cost_estimate=pl.CostEstimate(
            flops=2**20, bytes_accessed=8 * 2**20, transcendentals=0
        ),
    )(rows, mask_rows)


def order_tables(order_ref):
    row = lax.broadcasted_iota(jnp.int32, (ROWS, ROWS), 0)
    column = lane_ids((ROWS, ROWS))
    forth = (((row & 31) << 3) | (row >> 5)) == column
    back = (((row & 7) << 5) | (row >> 3)) == column
    order_ref[0] = forth.astype(F32).astype(BF16)
    order_ref[1] = back.astype(F32).astype(BF16)


def moved_rows(order, value):
    both = jnp.concatenate(split(value), axis=1)
    return jnp.dot(order, both, preferred_element_type=F32)


def sides(p_ref, f_hi, f_lo):
    def spread(which, sources, targets):
        blocks = [f[y, z] for f in (f_hi, f_lo) for y, z in sources]
        moved = jnp.dot(
            p_ref[which], jnp.concatenate(blocks, axis=1), preferred_element_type=F32
        )
        n = 0
        for f in (f_hi, f_lo):
            for y, z in targets:
                f[y, z] = moved[:, n * 128 : (n + 1) * 128].astype(BF16)
                n += 1

    inner = range(1, 9)
    spread(0, [(8, z) for z in inner], [(0, z) for z in inner])
    spread(1, [(1, z) for z in inner], [(9, z) for z in inner])
    spread(2, [(y, 8) for y in range(10)], [(y, 0) for y in range(10)])
    spread(3, [(y, 1) for y in range(10)], [(y, 9) for y in range(10)])


def put(f_hi, f_lo, y, hi, lo):
    f_hi[y + 1, 1:9] = hi.astype(BF16).reshape(8, SLOTS, 128)
    f_lo[y + 1, 1:9] = lo.astype(BF16).reshape(8, SLOTS, 128)


def fill_mid(i, v_ref, order_ref, f_hi, f_lo):
    upper = lane_ids((ROWS, 128)) < 32 + 64 * i

    def one(y, carry):
        v0 = tile_rows(v_ref, y)
        v1 = tile_rows(v_ref, 8 + y)
        moved = moved_rows(order_ref[0], jnp.where(upper, v1, v0))
        put(f_hi, f_lo, y, moved[:, :128], moved[:, 128:])
        return carry

    lax.fori_loop(0, 8, one, 0, unroll=8)


def fill_ends(i, v_ref, px_ref, up, down, low, high, order_ref, halo, f_hi, f_lo):
    outer = lane_ids((ROWS, 128)) // 32 == 3 - 3 * i
    for q in range(2):
        near = jnp.where(i == 0, up[0, q], down[0, q])
        far = jnp.where(i == 0, low[0, q], high[0, q])
        halo[q] = moved_rows(px_ref[0], jnp.concatenate([near, far], axis=0))

    def one(q, carry):
        for g in range(4):
            y = q * 4 + g
            moved = moved_rows(order_ref[0], tile_rows(v_ref, 8 * i + y))
            parts = []
            for part in range(2):
                side = halo[q, :, 128 * part : 128 * part + 128]
                side = pltpu.roll(side, 128 - 32 * g, 1) if g else side
                parts.append(
                    jnp.where(outer, side, moved[:, 128 * part : 128 * part + 128])
                )
            put(f_hi, f_lo, y, *parts)
        return carry

    lax.fori_loop(0, 2, one, 0, unroll=2)


def inner_rows(m, y, r_ref, m_ref):
    group = lane_ids((ROWS, 128)) // 32
    every = slice(None)
    a = masked(r_ref, m_ref, every, y)
    b = masked(r_ref, m_ref, every, 8 + y % 4)
    b = pltpu.roll(b, 64, 1) if y > 3 else b
    return jnp.where((m >= 2) & ((group == 1) | (group == 2)), b, a)


def fill_inner(m, r_ref, m_ref, order_ref, f_hi, f_lo):
    for y in range(8):
        moved = moved_rows(order_ref[0], inner_rows(m, y, r_ref, m_ref))
        put(f_hi, f_lo, y, moved[:, :128], moved[:, 128:])


def fill_outer(m, r_ref, m_ref, px_ref, up, down, low, high, order_ref, halo, f_hi, f_lo):
    group = lane_ids((ROWS, 128)) // 32
    outer = group == jnp.where(m == 0, 3, 0)
    edge = group == jnp.where(m == 0, 0, 3)
    for q in range(2):
        own = jnp.where(m == 0, down[0, q], up[0, q])
        near = jnp.where(m == 0, up[0, q], down[0, q])
        far = jnp.where(m == 0, low[0, q], high[0, q])
        halo[q] = moved_rows(px_ref[0], jnp.concatenate([near, far], axis=0))
        halo[2 + q] = moved_rows(order_ref[0], own)
    for y in range(8):
        q, g = y // 4, y % 4
        moved = moved_rows(order_ref[0], inner_rows(m, y, r_ref, m_ref))
        parts = []
        for part in range(2):
            lanes = slice(128 * part, 128 * part + 128)
            side, own = halo[q, :, lanes], halo[2 + q, :, lanes]
            if g:
                side = pltpu.roll(side, 128 - 32 * g, 1)
                own = pltpu.roll(own, 128 - 32 * g, 1)
            value = jnp.where(outer, side, moved[:, lanes])
            parts.append(jnp.where(edge, own, value))
        put(f_hi, f_lo, y, *parts)


def convolve(f_hi, f_lo, w_ref, store, beside=lambda t: None):
    for t in range(4):
        parts = []
        for j in range(3):
            for k in range(3):
                for f in (f_hi, f_lo):
                    rows = f[2 * t + j : 2 * t + j + 2, k : k + 8]
                    parts.append(rows.reshape(2 * ROWS, 128))
        both = jnp.dot(
            jnp.concatenate(parts, axis=1), w_ref[0, 0], preferred_element_type=F32
        )
        beside(t)
        for d in range(2):
            at = slice(d * ROWS, (d + 1) * ROWS)
            store(2 * t + d, both[at, :128] + both[at, 128:])


def by_brick(order_ref, sum_ref, acc_ref):
    for y in range(8):
        back = moved_rows(order_ref[1], sum_ref[y * ROWS : (y + 1) * ROWS, :])
        acc_ref[:, y] = (back[:, :128] + back[:, 128:]).reshape(SLOTS, 8, 128)


def finish_pair(n, acc_ref, occ_ref, bias, out_ref):
    low = lane_ids((64, 128)) < 64
    b = 2 * n
    t = acc_ref[b : b + 2].reshape(128, 128).T
    even, odd = t[:64], t[64:]
    first = jnp.where(low, even, pltpu.roll(odd, 64, 1))
    second = jnp.where(low, pltpu.roll(even, 64, 1), odd)
    for d, value in enumerate((first, second)):
        mask = occ_ref[b + d : b + d + 1, :].astype(F32)
        out_ref[b + d] = mask * jnp.maximum(value + bias, 0.0)


def early_body(mid, refs):
    i = pl.program_id(0)
    v_ref, p_ref, w_ref, *refs = refs
    extra = []
    if not mid:
        extra, refs = refs[:5], refs[5:]
    out_ref, f_hi, f_lo, order_ref, halo = refs

    @pl.when(i == 0)
    def _():
        order_tables(order_ref)

    if mid:
        fill_mid(i, v_ref, order_ref, f_hi, f_lo)
    else:
        fill_ends(i, v_ref, *extra, order_ref, halo, f_hi, f_lo)
    sides(p_ref, f_hi, f_lo)

    def store(y, value):
        out_ref[0, y * ROWS : (y + 1) * ROWS, :] = value

    convolve(f_hi, f_lo, w_ref, store)


def late_body(*refs):
    r_ref, m_ref, p_ref, w_ref, *refs = refs
    sides_refs, refs = refs[:5], refs[5:]
    acc_mid, acc_ends, occ_ref, bias_ref, out_ref, *refs = refs
    f_hi, f_lo, order_ref, halo, sum_ref, acc_ref = refs
    m = pl.program_id(0)
    mid = (m == 1) | (m == 2)

    @pl.when(m == 0)
    def _():
        order_tables(order_ref)

    @pl.when(mid)
    def _():
        fill_inner(m, r_ref, m_ref, order_ref, f_hi, f_lo)

    @pl.when((m == 0) | (m == 3))
    def _():
        fill_outer(m, r_ref, m_ref, *sides_refs, order_ref, halo, f_hi, f_lo)

    def store(y, value):
        at = slice(y * ROWS, (y + 1) * ROWS)
        sum_ref[at, :] = value + jnp.where(mid, acc_mid[0, at, :], acc_ends[0, at, :])

    def before(t):
        bias = bias_ref[...]
        for n in range(4 * t, 4 * t + 4):
            finish_pair(n, acc_ref, occ_ref, bias, out_ref)

    @pl.when(m < 4)
    def _():
        sides(p_ref, f_hi, f_lo)
        convolve(f_hi, f_lo, w_ref, store, before)
        by_brick(order_ref, sum_ref, acc_ref)

    @pl.when(m == 4)
    def _():
        for t in range(4):
            before(t)


VMEM = pl.BlockSpec(memory_space=pltpu.VMEM)
FIELDS = [pltpu.VMEM((10, 10, SLOTS, 128), BF16)] * 2 + [pltpu.VMEM((2, ROWS, ROWS), BF16)]
PARAMS = pltpu.CompilerParams(vmem_limit_bytes=GRANT)


def half_of(h):
    return pl.BlockSpec((1, 2, ROWS, 128), lambda i: (h, 0, 0, 0))


def early(mid, rows, perms, weights, ends=()):
    kind = (lambda i: 1 - i) if mid else (lambda i: i)
    operands = [rows, perms, weights]
    specs = [VMEM, VMEM, pl.BlockSpec((1, 1, 18 * 128, 256), lambda i: (0, kind(i), 0, 0))]
    if not mid:
        operands += list(ends)
        specs += [pl.BlockSpec((1, ROWS, 2 * ROWS), lambda i: (i, 0, 0))] + [half_of(0)] * 4
    return pl.pallas_call(
        lambda *refs: early_body(mid, refs),
        out_shape=jax.ShapeDtypeStruct((2, 64 * SLOTS, 128), F32),
        grid=(2,),
        in_specs=specs,
        out_specs=pl.BlockSpec((1, 64 * SLOTS, 128), lambda i: (i, 0, 0)),
        scratch_shapes=FIELDS + [pltpu.VMEM((2, ROWS, ROWS), F32)],
        compiler_params=PARAMS,
        name="mid" if mid else "ends",
        cost_estimate=pl.CostEstimate(
            flops=2 * 2 * 2048 * 2304 * 256, bytes_accessed=8 * 2**20, transcendentals=0
        ),
    )(*operands)


def late(rows, mask_rows, perms, weights, ends, kept_mid, kept_ends, occupancy, bias):
    acc = (1, 64 * SLOTS, 128)
    specs = [VMEM, VMEM, VMEM]
    specs += [pl.BlockSpec((1, 1, 18 * 128, 256), lambda m: (1, m % 2, 0, 0))]
    specs += [pl.BlockSpec((1, ROWS, 2 * ROWS), lambda m: (jnp.minimum(m // 2, 1), 0, 0))]
    specs += [half_of(1)] * 4
    specs += [pl.BlockSpec(acc, lambda m: (jnp.minimum(m // 2, 1), 0, 0))]
    specs += [pl.BlockSpec(acc, lambda m: (m // 3, 0, 0))]
    specs += [pl.BlockSpec((SLOTS, 128), lambda m: (0, jnp.maximum(m - 1, 0))), VMEM]
    return pl.pallas_call(
        lambda *refs: late_body(*refs),
        out_shape=jax.ShapeDtypeStruct((SLOTS, 64, 512), F32),
        grid=(5,),
        in_specs=specs,
        out_specs=pl.BlockSpec((SLOTS, 64, 128), lambda m: (0, 0, jnp.maximum(m - 1, 0))),
        scratch_shapes=FIELDS
        + [
            pltpu.VMEM((4, ROWS, ROWS), F32),
            pltpu.VMEM(acc[1:], F32),
            pltpu.VMEM((SLOTS, 8, 8, 128), F32),
        ],
        compiler_params=PARAMS,
        name="late",
        cost_estimate=pl.CostEstimate(
            flops=4 * 2 * 2048 * 2304 * 256, bytes_accessed=16 * 2**20, transcendentals=0
        ),
    )(rows, mask_rows, perms, weights, *ends, kept_mid, kept_ends, occupancy, bias)


def mask_kernel(occ_ref, first_ref, second_ref):
    group = lax.broadcasted_iota(jnp.int32, (8, 128), 0)
    spread = (lane_ids((8, 128)) // 32 == group).astype(F32)

    def one(b, carry):
        rows = jnp.dot(occ_ref[b].T, spread, preferred_element_type=F32)
        first_ref[b] = rows[:160].reshape(20, 8, 128)
        second_ref[b] = rows[160:].reshape(12, 8, 128)
        return carry

    lax.fori_loop(0, SLOTS, one, 0, unroll=2)


def mask_tables(occupancy):
    occ = occupancy.astype(F32).reshape(SLOTS, 8, 64)
    base = occ.reshape(SLOTS, 2, 4, 64).transpose(0, 2, 1, 3).reshape(SLOTS, 4, 128)
    faces = occ.reshape(SLOTS, 8, 2, 4, 8)
    up = jnp.roll(faces[:, 7].transpose(0, 2, 1, 3), 3, axis=1)
    down = faces[:, 0].transpose(0, 2, 1, 3)
    a = jnp.concatenate([occ[:, 4:5], occ[:, 1:4]], axis=1)
    b = jnp.stack(
        [occ[:, 6, 32:], occ[:, 5, :32], occ[:, 6, :32], occ[:, 5, 32:]], axis=1
    )
    packed = [base, up.reshape(SLOTS, 4, 16), down.reshape(SLOTS, 4, 16), a, b]
    packed = jnp.pad(jnp.concatenate(packed, axis=2), ((0, 0), (0, 4), (0, 0)))
    return pl.pallas_call(
        mask_kernel,
        out_shape=(
            jax.ShapeDtypeStruct((SLOTS, 20, 8, 128), F32),
            jax.ShapeDtypeStruct((SLOTS, 12, 8, 128), F32),
        ),
        name="masks",
        compiler_params=pltpu.CompilerParams(vmem_limit_bytes=GRANT),
        cost_estimate=pl.CostEstimate(
            flops=2**20, bytes_accessed=4 * 2**20, transcendentals=0
        ),
    )(packed)


def weight_kernel(w_ref, out_ref):
    h = pl.program_id(0)
    row = lax.broadcasted_iota(jnp.int32, (32, 128), 0) + 32 * h
    lanes = lane_ids((32, 128))
    low = lanes < 64
    eye = (lanes % 64 == row).astype(F32)
    zero = jnp.zeros((32, 128), F32)
    channels = pl.ds(pl.multiple_of(32 * h, 32), 32)
    for jk in range(9):
        taps = [w_ref[9 * i + jk, channels, :] for i in range(3)]
        if jk == 4:
            taps[1] = taps[1] + eye
        taps = taps + [zero]
        window = [split(jnp.where(low, taps[d], taps[d - 1])) for d in range(4)]
        for kind, order in enumerate(((1, 2, 3, 0), (3, 0, 1, 2))):
            hi = jnp.concatenate([window[d][0] for d in order], axis=0)
            lo = jnp.concatenate([window[d][1] for d in order], axis=0)
            at = 256 * jk
            out_ref[0, kind, at : at + 128, :128] = hi
            out_ref[0, kind, at : at + 128, 128:] = lo
            out_ref[0, kind, at + 128 : at + 256, :128] = lo
            out_ref[0, kind, at + 128 : at + 256, 128:] = hi


def weight_tables(weights):
    w = weights.reshape(27, 64, 64)
    return pl.pallas_call(
        weight_kernel,
        out_shape=jax.ShapeDtypeStruct((2, 2, 18 * 128, 256), BF16),
        grid=(2,),
        in_specs=[pl.BlockSpec(memory_space=pltpu.VMEM)],
        out_specs=pl.BlockSpec((1, 2, 18 * 128, 256), lambda h: (h, 0, 0, 0)),
        name="weights",
        compiler_params=pltpu.CompilerParams(vmem_limit_bytes=GRANT),
        cost_estimate=pl.CostEstimate(
            flops=2**20, bytes_accessed=6 * 2**20, transcendentals=0
        ),
    )(jnp.concatenate([w, w], axis=2))


def owner(receive, occupancy, neighbours, own_rank, weight_one, bias_one, shift):
    mask_first, mask_second = mask_tables(occupancy)
    tables = weight_tables(weight_one)
    bias = jnp.broadcast_to(bias_one[:, None], (64, 128))
    present = neighbours >= 0
    local = neighbours % SLOTS
    away = (neighbours // SLOTS != own_rank).astype(jnp.int32) * SLOTS
    ids = jnp.where(present, local, -1)
    slots = jnp.arange(SLOTS, dtype=jnp.int32)
    perms = (ids[:, 2:].T[:, :, None] == slots).astype(BF16)
    wide = jnp.where(present, local + away, -SLOTS * 8)[:, :2].T[:, None, :] * 8
    wide = wide + jnp.arange(8, dtype=jnp.int32)[:, None]
    places = jnp.arange(2 * ROWS, dtype=jnp.int32)
    perms_x = (wide.reshape(2, ROWS)[:, :, None] == places).astype(BF16)
    rows = receive(0, ()).reshape(SLOTS, 20, 8, 128)
    ready = (mask_first, mask_second, tables, perms, perms_x, bias)
    later = receive(1, ready).reshape(SLOTS, 12, 8, 128)
    rows, up, down = planes(rows, mask_first)
    ends = (perms_x, up, down, shift(up, 1), shift(down, -1))
    kept_mid = early(True, rows, perms, tables)
    kept_ends = early(False, rows, perms, tables, ends)
    return late(
        later, mask_second, perms, tables, ends, kept_mid, kept_ends, occupancy, bias
    )


def shards(features, send_pick, occupancy, neighbours, weight_one, bias_one):
    def receive(h, after):
        outgoing = pack(h, send_pick, features, after)
        return lax.all_to_all(outgoing, "gx", split_axis=0, concat_axis=0, tiled=True)

    def shift(block, distance):
        return passed_along(block, ("gx", "gy"), distance)

    own_rank = lax.axis_index(("gx", "gy"))
    return owner(
        receive,
        occupancy,
        neighbours,
        own_rank,
        weight_one,
        bias_one,
        shift,
    )


def solution(mesh):
    in_specs = (
        P(("gx", "gy"), None, None),
        P(("gx", "gy"), None),
        P(("gx", "gy"), None),
        P(("gx", "gy"), None),
        P(),
        P(),
    )
    out_specs = P(("gx", "gy"), None, None)
    return jax.shard_map(
        shards, mesh=mesh, in_specs=in_specs, out_specs=out_specs, check_vma=False
    )
```

```python
import jax
import jax.numpy as jnp
from jax import lax
from jax.experimental import pallas as pl
from jax.experimental.pallas import tpu as pltpu
from jax.sharding import PartitionSpec as P


F32 = jnp.float32
BF16 = jnp.bfloat16
SLOTS = 32
SRC = 16
ROWS = 8 * SLOTS
GRANT = 67043328
PACK = 8
PLANE = 16


def passed_along(block, axis, distance):
    devices = range(lax.axis_size(axis))
    route = [(i - distance, i) for i in devices if i - distance in devices]
    return lax.ppermute(block, axis, route)


def lane_ids(shape):
    return lax.broadcasted_iota(jnp.int32, shape, len(shape) - 1)


def split(v):
    hi = v.astype(BF16)
    return hi, (v - hi.astype(F32)).astype(BF16)


def turned(x_ref, r, channels):
    low = lane_ids((32, 128)) < 64
    groups = []
    for g in range(4):
        p = g // 2
        a = x_ref[r, channels, p * 128 : (p + 1) * 128]
        b = x_ref[r, channels, (p + 2) * 128 : (p + 3) * 128]
        if g % 2 == 0:
            groups.append(jnp.where(low, a, pltpu.roll(b, 64, 1)))
        else:
            groups.append(jnp.where(low, pltpu.roll(a, 64, 1), b))
    return jnp.concatenate(groups, axis=0).T


def pack_first(x_ref, t_ref):
    channels = slice(32, 64)
    low = lane_ids((32, 128)) < 64
    group = lane_ids((8, 128)) // 32
    for first in range(0, PACK, 4):
        both = []
        for r in range(first, first + 4):
            t_ref[r, :128] = turned(x_ref, r, slice(0, 32))
            both.append(
                jnp.where(low, x_ref[r, channels, :128], x_ref[r, channels, 384:])
            )
        planes_t = jnp.concatenate(both, axis=0).T
        for r in range(4):
            for plane in range(2):
                for q in range(2):
                    value = None
                    for g in range(4):
                        at = (1 - plane) * 64 + (4 * q + g) * 8
                        to = (g + 3) % 4 if plane == 0 else g
                        tile = planes_t[at : at + 8]
                        if to != r:
                            tile = pltpu.roll(tile, (32 * (to - r)) % 128, 1)
                        if value is not None:
                            tile = jnp.where(group == to, tile, value)
                        value = tile
                    at = 128 + (2 * plane + q) * 8
                    t_ref[first + r, at : at + 8] = value


def pack_second(x_ref, t_ref):
    group = lane_ids((64, 128)) // 32
    group_b = lane_ids((32, 128)) // 32
    inner = (group_b == 1) | (group_b == 2)
    for r in range(PACK):
        t = turned(x_ref, r, slice(32, 64))
        t_ref[r, :64] = jnp.where(group == 0, t[64:], t[:64])
        t_ref[r, 64:96] = jnp.where(inner, t[64:96], pltpu.roll(t[96:], 64, 1))


def pack_kernel(half, pick_ref, x_ref, *refs):
    out_ref, t_ref, slot_ref, sem = refs[-4:]
    n = pl.program_id(0)

    @pl.when(n == 0)
    def _():
        for j in range(SLOTS):
            p = pick_ref[0, j]
            slot_ref[jnp.where(p < 0, SRC, p)] = j

    (pack_second if half else pack_first)(x_ref, t_ref.at[pl.ds(PACK * n, PACK)])

    def copy(r):
        return pltpu.make_async_copy(t_ref.at[r], out_ref.at[slot_ref[r]], sem.at[r])

    for r in range(PACK):
        copy(PACK * n + r).start()

    @pl.when(n == SRC // PACK - 1)
    def _():
        for r in range(SRC):
            copy(r).wait()


def pack(half, send_pick, features, after):
    rows = 96 if half else 160
    return pl.pallas_call(
        lambda *refs: pack_kernel(half, *refs),
        out_shape=jax.ShapeDtypeStruct((SLOTS, rows, 128), F32),
        grid=(SRC // PACK,),
        in_specs=[
            pl.BlockSpec(memory_space=pltpu.SMEM),
            pl.BlockSpec((PACK, 64, 512), lambda n: (n, 0, 0)),
        ]
        + [pl.BlockSpec(memory_space=pl.ANY)] * len(after),
        out_specs=pl.BlockSpec(memory_space=pl.ANY),
        scratch_shapes=[
            pltpu.VMEM((SRC, rows, 128), F32),
            pltpu.SMEM((SLOTS,), jnp.int32),
            pltpu.SemaphoreType.DMA((SRC,)),
        ],
        compiler_params=pltpu.CompilerParams(vmem_limit_bytes=GRANT),
        cost_estimate=pl.CostEstimate(
            flops=0, bytes_accessed=6 * 2**20, transcendentals=0
        ),
    )(send_pick, features, *after)


def masked(r_ref, m_ref, at, tile):
    rows = jnp.where(m_ref[at, tile] > 0, r_ref[at, tile], 0.0)
    return rows.reshape(rows.shape[0] * 8, 128)


def tile_rows(v_ref, tile):
    return masked(*v_ref, slice(None), tile)


def planes_kernel(r_ref, m_ref, up_ref, down_ref):
    group = lane_ids((32, 128)) // 32

    for c in range(PLANE // 4):
        bricks = slice(c * 4, c * 4 + 4)
        out = slice(c * 32, c * 32 + 32)
        for q in range(2):
            up = jnp.zeros((32, 128), F32)
            down = jnp.zeros((32, 128), F32)
            for g in range(4):
                tile = 4 * q + g
                v0 = r_ref[bricks, tile].reshape(32, 128)
                v1 = r_ref[bricks, tile + 8].reshape(32, 128)
                v0 = pltpu.roll(v0, 32 * g, 1) if g else v0
                v1 = pltpu.roll(v1, 32 * g, 1) if g else v1
                up = jnp.where(group == (g + 3) % 4, v1, up)
                down = jnp.where(group == g, v0, down)
            there = m_ref[bricks, q].reshape(32, 128) > 0
            up_ref[0, q, out, :] = jnp.where(there, up, 0.0)
            far = r_ref[bricks, 16 + q].reshape(32, 128)
            up_ref[1, q, out, :] = jnp.where(there, far, 0.0)
            there = m_ref[bricks, 2 + q].reshape(32, 128) > 0
            down_ref[0, q, out, :] = jnp.where(there, down, 0.0)
            far = r_ref[bricks, 18 + q].reshape(32, 128)
            down_ref[1, q, out, :] = jnp.where(there, far, 0.0)


def planes(rows, mask_rows):
    shape = jax.ShapeDtypeStruct((2, 2, ROWS, 128), F32)
    tiles = pl.BlockSpec((PLANE, 20, 8, 128), lambda n: (n, 0, 0, 0))
    faces = pl.BlockSpec((PLANE, 4, 8, 128), lambda n: (n, 4, 0, 0))
    plane = pl.BlockSpec((2, 2, 8 * PLANE, 128), lambda n: (0, 0, n, 0))
    return pl.pallas_call(
        planes_kernel,
        out_shape=(shape, shape),
        grid=(SLOTS // PLANE,),
        in_specs=[tiles, faces],
        out_specs=(plane, plane),
        name="planes",
        compiler_params=pltpu.CompilerParams(vmem_limit_bytes=GRANT),
        cost_estimate=pl.CostEstimate(
            flops=2**20, bytes_accessed=8 * 2**20, transcendentals=0
        ),
    )(rows, mask_rows)


def order_tables(order_ref):
    row = lax.broadcasted_iota(jnp.int32, (ROWS, ROWS), 0)
    column = lane_ids((ROWS, ROWS))
    forth = (((row & 31) << 3) | (row >> 5)) == column
    back = (((row & 7) << 5) | (row >> 3)) == column
    order_ref[0] = forth.astype(F32).astype(BF16)
    order_ref[1] = back.astype(F32).astype(BF16)


def moved_rows(order, value):
    both = jnp.concatenate(split(value), axis=1)
    return jnp.dot(order, both, preferred_element_type=F32)


def sides(p_ref, f_hi, f_lo):
    def spread(which, sources, targets):
        blocks = [f[y, z] for f in (f_hi, f_lo) for y, z in sources]
        moved = jnp.dot(
            p_ref[which], jnp.concatenate(blocks, axis=1), preferred_element_type=F32
        )
        n = 0
        for f in (f_hi, f_lo):
            for y, z in targets:
                f[y, z] = moved[:, n * 128 : (n + 1) * 128].astype(BF16)
                n += 1

    inner = range(1, 9)
    spread(0, [(8, z) for z in inner], [(0, z) for z in inner])
    spread(1, [(1, z) for z in inner], [(9, z) for z in inner])
    spread(2, [(y, 8) for y in range(10)], [(y, 0) for y in range(10)])
    spread(3, [(y, 1) for y in range(10)], [(y, 9) for y in range(10)])


def put(f_hi, f_lo, y, hi, lo):
    f_hi[y + 1, 1:9] = hi.astype(BF16).reshape(8, SLOTS, 128)
    f_lo[y + 1, 1:9] = lo.astype(BF16).reshape(8, SLOTS, 128)


def fill_mid(i, v_ref, order_ref, f_hi, f_lo):
    upper = lane_ids((ROWS, 128)) < 32 + 64 * i

    def one(y, carry):
        v0 = tile_rows(v_ref, y)
        v1 = tile_rows(v_ref, 8 + y)
        moved = moved_rows(order_ref[0], jnp.where(upper, v1, v0))
        put(f_hi, f_lo, y, moved[:, :128], moved[:, 128:])
        return carry

    lax.fori_loop(0, 8, one, 0, unroll=8)


def fill_ends(i, v_ref, px_ref, up, down, low, high, order_ref, halo, f_hi, f_lo):
    outer = lane_ids((ROWS, 128)) // 32 == 3 - 3 * i
    for q in range(2):
        near = jnp.where(i == 0, up[0, q], down[0, q])
        far = jnp.where(i == 0, low[0, q], high[0, q])
        halo[q] = moved_rows(px_ref[0], jnp.concatenate([near, far], axis=0))

    def one(q, carry):
        for g in range(4):
            y = q * 4 + g
            moved = moved_rows(order_ref[0], tile_rows(v_ref, 8 * i + y))
            parts = []
            for part in range(2):
                side = halo[q, :, 128 * part : 128 * part + 128]
                side = pltpu.roll(side, 128 - 32 * g, 1) if g else side
                parts.append(
                    jnp.where(outer, side, moved[:, 128 * part : 128 * part + 128])
                )
            put(f_hi, f_lo, y, *parts)
        return carry

    lax.fori_loop(0, 2, one, 0, unroll=2)


def inner_rows(m, y, r_ref, m_ref):
    group = lane_ids((ROWS, 128)) // 32
    every = slice(None)
    a = masked(r_ref, m_ref, every, y)
    b = masked(r_ref, m_ref, every, 8 + y % 4)
    b = pltpu.roll(b, 64, 1) if y > 3 else b
    return jnp.where((m >= 2) & ((group == 1) | (group == 2)), b, a)


def fill_inner(m, r_ref, m_ref, order_ref, f_hi, f_lo):
    for y in range(8):
        moved = moved_rows(order_ref[0], inner_rows(m, y, r_ref, m_ref))
        put(f_hi, f_lo, y, moved[:, :128], moved[:, 128:])


def fill_outer(m, r_ref, m_ref, px_ref, up, down, low, high, order_ref, halo, f_hi, f_lo):
    group = lane_ids((ROWS, 128)) // 32
    outer = group == jnp.where(m == 0, 3, 0)
    edge = group == jnp.where(m == 0, 0, 3)
    for q in range(2):
        own = jnp.where(m == 0, down[0, q], up[0, q])
        near = jnp.where(m == 0, up[0, q], down[0, q])
        far = jnp.where(m == 0, low[0, q], high[0, q])
        halo[q] = moved_rows(px_ref[0], jnp.concatenate([near, far], axis=0))
        halo[2 + q] = moved_rows(order_ref[0], own)
    for y in range(8):
        q, g = y // 4, y % 4
        moved = moved_rows(order_ref[0], inner_rows(m, y, r_ref, m_ref))
        parts = []
        for part in range(2):
            lanes = slice(128 * part, 128 * part + 128)
            side, own = halo[q, :, lanes], halo[2 + q, :, lanes]
            if g:
                side = pltpu.roll(side, 128 - 32 * g, 1)
                own = pltpu.roll(own, 128 - 32 * g, 1)
            value = jnp.where(outer, side, moved[:, lanes])
            parts.append(jnp.where(edge, own, value))
        put(f_hi, f_lo, y, *parts)


def convolve(f_hi, f_lo, w_ref, store, beside=lambda t: None):
    for t in range(4):
        parts = []
        for j in range(3):
            for k in range(3):
                for f in (f_hi, f_lo):
                    rows = f[2 * t + j : 2 * t + j + 2, k : k + 8]
                    parts.append(rows.reshape(2 * ROWS, 128))
        both = jnp.dot(
            jnp.concatenate(parts, axis=1), w_ref[0, 0], preferred_element_type=F32
        )
        beside(t)
        for d in range(2):
            at = slice(d * ROWS, (d + 1) * ROWS)
            store(2 * t + d, both[at, :128] + both[at, 128:])


def by_brick(order_ref, sum_ref, acc_ref):
    for y in range(8):
        back = moved_rows(order_ref[1], sum_ref[y * ROWS : (y + 1) * ROWS, :])
        acc_ref[:, y] = (back[:, :128] + back[:, 128:]).reshape(SLOTS, 8, 128)


def finish_pair(n, acc_ref, occ_ref, bias, out_ref):
    low = lane_ids((64, 128)) < 64
    b = 2 * n
    t = acc_ref[b : b + 2].reshape(128, 128).T
    even, odd = t[:64], t[64:]
    first = jnp.where(low, even, pltpu.roll(odd, 64, 1))
    second = jnp.where(low, pltpu.roll(even, 64, 1), odd)
    for d, value in enumerate((first, second)):
        mask = occ_ref[b + d : b + d + 1, :].astype(F32)
        out_ref[b + d] = mask * jnp.maximum(value + bias, 0.0)


def early_body(mid, refs):
    i = pl.program_id(0)
    r_ref, m_ref, p_ref, w_ref, *refs = refs
    v_ref = (r_ref, m_ref)
    extra = []
    if not mid:
        extra, refs = refs[:5], refs[5:]
    out_ref, f_hi, f_lo, order_ref, halo = refs

    @pl.when(i == 0)
    def _():
        order_tables(order_ref)

    if mid:
        fill_mid(i, v_ref, order_ref, f_hi, f_lo)
    else:
        fill_ends(i, v_ref, *extra, order_ref, halo, f_hi, f_lo)
    sides(p_ref, f_hi, f_lo)

    def store(y, value):
        out_ref[0, y * ROWS : (y + 1) * ROWS, :] = value

    convolve(f_hi, f_lo, w_ref, store)


def late_body(*refs):
    r_ref, m_ref, p_ref, w_ref, *refs = refs
    sides_refs, refs = refs[:5], refs[5:]
    acc_mid, acc_ends, occ_ref, bias_ref, out_ref, *refs = refs
    f_hi, f_lo, order_ref, halo, sum_ref, acc_ref = refs
    m = pl.program_id(0)
    mid = (m == 1) | (m == 2)

    @pl.when(m == 0)
    def _():
        order_tables(order_ref)

    @pl.when(mid)
    def _():
        fill_inner(m, r_ref, m_ref, order_ref, f_hi, f_lo)

    @pl.when((m == 0) | (m == 3))
    def _():
        fill_outer(m, r_ref, m_ref, *sides_refs, order_ref, halo, f_hi, f_lo)

    def store(y, value):
        at = slice(y * ROWS, (y + 1) * ROWS)
        sum_ref[at, :] = value + jnp.where(mid, acc_mid[0, at, :], acc_ends[0, at, :])

    def before(t):
        bias = bias_ref[...]
        for n in range(4 * t, 4 * t + 4):
            finish_pair(n, acc_ref, occ_ref, bias, out_ref)

    @pl.when(m < 4)
    def _():
        sides(p_ref, f_hi, f_lo)
        convolve(f_hi, f_lo, w_ref, store, before)
        by_brick(order_ref, sum_ref, acc_ref)

    @pl.when(m == 4)
    def _():
        for t in range(4):
            before(t)


VMEM = pl.BlockSpec(memory_space=pltpu.VMEM)
FIELDS = [pltpu.VMEM((10, 10, SLOTS, 128), BF16)] * 2 + [pltpu.VMEM((2, ROWS, ROWS), BF16)]
PARAMS = pltpu.CompilerParams(vmem_limit_bytes=GRANT)


def half_of(h):
    return pl.BlockSpec((1, 2, ROWS, 128), lambda i: (h, 0, 0, 0))


def early(mid, rows, mask_rows, perms, weights, ends=()):
    kind = (lambda i: 1 - i) if mid else (lambda i: i)
    operands = [rows, mask_rows, perms, weights]
    specs = [VMEM] * 3 + [pl.BlockSpec((1, 1, 18 * 128, 256), lambda i: (0, kind(i), 0, 0))]
    if not mid:
        operands += list(ends)
        specs += [pl.BlockSpec((1, ROWS, 2 * ROWS), lambda i: (i, 0, 0))] + [half_of(0)] * 4
    return pl.pallas_call(
        lambda *refs: early_body(mid, refs),
        out_shape=jax.ShapeDtypeStruct((2, 64 * SLOTS, 128), F32),
        grid=(2,),
        in_specs=specs,
        out_specs=pl.BlockSpec((1, 64 * SLOTS, 128), lambda i: (i, 0, 0)),
        scratch_shapes=FIELDS + [pltpu.VMEM((2, ROWS, ROWS), F32)],
        compiler_params=PARAMS,
        name="mid" if mid else "ends",
        cost_estimate=pl.CostEstimate(
            flops=2 * 2 * 2048 * 2304 * 256, bytes_accessed=8 * 2**20, transcendentals=0
        ),
    )(*operands)


def late(rows, mask_rows, perms, weights, ends, kept_mid, kept_ends, occupancy, bias):
    acc = (1, 64 * SLOTS, 128)
    specs = [VMEM, VMEM, VMEM]
    specs += [pl.BlockSpec((1, 1, 18 * 128, 256), lambda m: (1, m % 2, 0, 0))]
    specs += [pl.BlockSpec((1, ROWS, 2 * ROWS), lambda m: (jnp.minimum(m // 2, 1), 0, 0))]
    specs += [half_of(1)] * 4
    specs += [pl.BlockSpec(acc, lambda m: (jnp.minimum(m // 2, 1), 0, 0))]
    specs += [pl.BlockSpec(acc, lambda m: (m // 3, 0, 0))]
    specs += [pl.BlockSpec((SLOTS, 128), lambda m: (0, jnp.maximum(m - 1, 0))), VMEM]
    return pl.pallas_call(
        lambda *refs: late_body(*refs),
        out_shape=jax.ShapeDtypeStruct((SLOTS, 64, 512), F32),
        grid=(5,),
        in_specs=specs,
        out_specs=pl.BlockSpec((SLOTS, 64, 128), lambda m: (0, 0, jnp.maximum(m - 1, 0))),
        scratch_shapes=FIELDS
        + [
            pltpu.VMEM((4, ROWS, ROWS), F32),
            pltpu.VMEM(acc[1:], F32),
            pltpu.VMEM((SLOTS, 8, 8, 128), F32),
        ],
        compiler_params=PARAMS,
        name="late",
        cost_estimate=pl.CostEstimate(
            flops=4 * 2 * 2048 * 2304 * 256, bytes_accessed=16 * 2**20, transcendentals=0
        ),
    )(rows, mask_rows, perms, weights, *ends, kept_mid, kept_ends, occupancy, bias)


def mask_kernel(occ_ref, first_ref, second_ref):
    group = lax.broadcasted_iota(jnp.int32, (8, 128), 0)
    spread = (lane_ids((8, 128)) // 32 == group).astype(F32)

    def one(b, carry):
        rows = jnp.dot(occ_ref[b].T, spread, preferred_element_type=F32)
        first_ref[b] = rows[:160].reshape(20, 8, 128)
        second_ref[b] = rows[160:].reshape(12, 8, 128)
        return carry

    lax.fori_loop(0, SLOTS, one, 0, unroll=2)


def mask_tables(occupancy):
    occ = occupancy.astype(F32).reshape(SLOTS, 8, 64)
    base = occ.reshape(SLOTS, 2, 4, 64).transpose(0, 2, 1, 3).reshape(SLOTS, 4, 128)
    faces = occ.reshape(SLOTS, 8, 2, 4, 8)
    up = jnp.roll(faces[:, 7].transpose(0, 2, 1, 3), 3, axis=1)
    down = faces[:, 0].transpose(0, 2, 1, 3)
    a = jnp.concatenate([occ[:, 4:5], occ[:, 1:4]], axis=1)
    b = jnp.stack(
        [occ[:, 6, 32:], occ[:, 5, :32], occ[:, 6, :32], occ[:, 5, 32:]], axis=1
    )
    packed = [base, up.reshape(SLOTS, 4, 16), down.reshape(SLOTS, 4, 16), a, b]
    packed = jnp.pad(jnp.concatenate(packed, axis=2), ((0, 0), (0, 4), (0, 0)))
    return pl.pallas_call(
        mask_kernel,
        out_shape=(
            jax.ShapeDtypeStruct((SLOTS, 20, 8, 128), F32),
            jax.ShapeDtypeStruct((SLOTS, 12, 8, 128), F32),
        ),
        name="masks",
        compiler_params=pltpu.CompilerParams(vmem_limit_bytes=GRANT),
        cost_estimate=pl.CostEstimate(
            flops=2**20, bytes_accessed=4 * 2**20, transcendentals=0
        ),
    )(packed)


def weight_kernel(w_ref, out_ref):
    h = pl.program_id(0)
    row = lax.broadcasted_iota(jnp.int32, (32, 128), 0) + 32 * h
    lanes = lane_ids((32, 128))
    low = lanes < 64
    eye = (lanes % 64 == row).astype(F32)
    zero = jnp.zeros((32, 128), F32)
    channels = pl.ds(pl.multiple_of(32 * h, 32), 32)
    for jk in range(9):
        taps = [w_ref[9 * i + jk, channels, :] for i in range(3)]
        if jk == 4:
            taps[1] = taps[1] + eye
        taps = taps + [zero]
        window = [split(jnp.where(low, taps[d], taps[d - 1])) for d in range(4)]
        for kind, order in enumerate(((1, 2, 3, 0), (3, 0, 1, 2))):
            hi = jnp.concatenate([window[d][0] for d in order], axis=0)
            lo = jnp.concatenate([window[d][1] for d in order], axis=0)
            at = 256 * jk
            out_ref[0, kind, at : at + 128, :128] = hi
            out_ref[0, kind, at : at + 128, 128:] = lo
            out_ref[0, kind, at + 128 : at + 256, :128] = lo
            out_ref[0, kind, at + 128 : at + 256, 128:] = hi


def weight_tables(weights):
    w = weights.reshape(27, 64, 64)
    return pl.pallas_call(
        weight_kernel,
        out_shape=jax.ShapeDtypeStruct((2, 2, 18 * 128, 256), BF16),
        grid=(2,),
        in_specs=[pl.BlockSpec(memory_space=pltpu.VMEM)],
        out_specs=pl.BlockSpec((1, 2, 18 * 128, 256), lambda h: (h, 0, 0, 0)),
        name="weights",
        compiler_params=pltpu.CompilerParams(vmem_limit_bytes=GRANT),
        cost_estimate=pl.CostEstimate(
            flops=2**20, bytes_accessed=6 * 2**20, transcendentals=0
        ),
    )(jnp.concatenate([w, w], axis=2))


def owner(receive, occupancy, neighbours, own_rank, weight_one, bias_one, shift):
    mask_first, mask_second = mask_tables(occupancy)
    tables = weight_tables(weight_one)
    bias = jnp.broadcast_to(bias_one[:, None], (64, 128))
    present = neighbours >= 0
    local = neighbours % SLOTS
    away = (neighbours // SLOTS != own_rank).astype(jnp.int32) * SLOTS
    ids = jnp.where(present, local, -1)
    slots = jnp.arange(SLOTS, dtype=jnp.int32)
    perms = (ids[:, 2:].T[:, :, None] == slots).astype(BF16)
    wide = jnp.where(present, local + away, -SLOTS * 8)[:, :2].T[:, None, :] * 8
    wide = wide + jnp.arange(8, dtype=jnp.int32)[:, None]
    places = jnp.arange(2 * ROWS, dtype=jnp.int32)
    perms_x = (wide.reshape(2, ROWS)[:, :, None] == places).astype(BF16)
    rows = receive(0, ()).reshape(SLOTS, 20, 8, 128)
    ready = (mask_first, mask_second, tables, perms, perms_x, bias)
    later = receive(1, ready).reshape(SLOTS, 12, 8, 128)
    up, down = planes(rows, mask_first)
    ends = (perms_x, up, down, shift(up, 1), shift(down, -1))
    kept_mid = early(True, rows, mask_first, perms, tables)
    kept_ends = early(False, rows, mask_first, perms, tables, ends)
    return late(
        later, mask_second, perms, tables, ends, kept_mid, kept_ends, occupancy, bias
    )


def shards(features, send_pick, occupancy, neighbours, weight_one, bias_one):
    def receive(h, after):
        outgoing = pack(h, send_pick, features, after)
        return lax.all_to_all(outgoing, "gx", split_axis=0, concat_axis=0, tiled=True)

    def shift(block, distance):
        return passed_along(block, ("gx", "gy"), distance)

    own_rank = lax.axis_index(("gx", "gy"))
    return owner(
        receive,
        occupancy,
        neighbours,
        own_rank,
        weight_one,
        bias_one,
        shift,
    )


def solution(mesh):
    in_specs = (
        P(("gx", "gy"), None, None),
        P(("gx", "gy"), None),
        P(("gx", "gy"), None),
        P(("gx", "gy"), None),
        P(),
        P(),
    )
    out_specs = P(("gx", "gy"), None, None)
    return jax.shard_map(
        shards, mesh=mesh, in_specs=in_specs, out_specs=out_specs, check_vma=False
    )
```
